128 devices in a mesh: bead: 4 (over z_lo, core), space: 32 (over z_hi, x, y).
Axes of the slice: x: 4, y: 4, z: 4 (z_hi: 2, z_lo: 2; z = z_hi * 2 + z_lo), core: 2. Of those that a mesh axis runs over, the one named last changes fastest.
Arguments:
- centroid: float32 [3, 65536], P(None, 'space'), may hold values from 0 to 1
- bead_offsets: float32 [32, 3, 65536], P('bead', None, 'space'), may hold values from -0.6 to 0.6
- routes: int32 [65536, 1], P('space'), may hold values from 0 to 31; in each aligned block of 2048 rows (0 to 2047, 2048 to 4095, ...) at most 128 rows name the same one
Outputs:
- forces: float32 [32, 3, 65536], P('bead', None, 'space')
The draws below stay inside these ranges and needn't reach their ends.
Inputs may be any that keep to these rules, and one draw needn't show every extreme that they name: `routes`: each molecule names one domain. The molecules of one slab name any one domain at most 128 times, a bound that some block reaches.
All inputs are finite; a program needn't handle non-finite values.
Results may differ from the reference program's by a relative error of at most 0.0003.
Values sent between devices are 32-bit elements; how exact they have to be, the bound alone decides.
No kernel may reach another device: no remote copies, remote signals or barrier semaphores. Data moves between devices by JAX's collectives and lax.ppermute only.
A program may use at most 64 MiB of HBM per device.

```python
import math
import jax
import jax.numpy as jnp
import numpy as np
from jax import lax

BEADS = 32
CONTRACTED = 4
M_DEV = 2048
MOLS = 65536
CAP = 128
SLOTS = 4096
N_SPACE = 32


def shard_levels(key, extent, cuts, low, top_value):
    factor_of = 1.0
    for position, blocks in cuts:
        steps = jax.random.uniform(jax.random.fold_in(jax.random.fold_in(key, 6), position), (blocks,), jnp.float32, low / len(cuts), top_value / len(cuts))
        factor_of = factor_of * jnp.repeat(jnp.exp(steps), extent[position] // blocks).reshape((-1,) + (1,) * (len(extent) - 1 - position))
    return factor_of


def shared_out(rng, own, number, rows, number_of, top, reach, lean):
    order = jax.random.permutation(rng, number_of)
    packed, common = shares(number_of, rows * top, reach, lean, True), shares(number_of, rows * top, reach, lean, False)
    places = jnp.arange(number_of)

    def named(tallies, turn):
        used = int((tallies > 0).sum())
        fixed = max(1, used // 4)
        shifted = fixed + (places - fixed + turn * (used - fixed)) % max(1, number_of - fixed)
        return jnp.zeros((number_of,), jnp.int32).at[order[jnp.where(places < fixed, places, shifted)]].set(jnp.asarray(tallies, jnp.int32))

    tallies = jnp.where(number % 4 == 0, named(packed, number // 4), named(common, number - number // 4 - 1))
    mixed = jax.random.permutation(jax.random.fold_in(own, 3), number_of)
    giver, sink = mixed[0:number_of // 2 * 2:2], mixed[1:number_of // 2 * 2:2]
    margin = jnp.minimum(tallies[giver] - 1, reach - tallies[sink]) // 2
    margin = jnp.where((giver == order[0]) | (sink == order[0]) | (tallies[sink] == 0), 0, jnp.maximum(margin, 0))
    shifted = jax.random.randint(jax.random.fold_in(own, 4), (number_of // 2,), 0, 1 << 20) % (margin + 1)
    tallies = tallies.at[giver].add(-shifted).at[sink].add(shifted)
    items = jnp.searchsorted(jnp.cumsum(tallies), jnp.arange(rows * top), side="right").astype(jnp.int32)
    listing = items.reshape(top, rows).T
    listing = listing[jax.random.permutation(jax.random.fold_in(own, 1), rows)]
    turn = jax.random.randint(jax.random.fold_in(own, 2), (rows, 1), 0, top)
    return jnp.take_along_axis(listing, (jnp.arange(top)[None, :] + turn) % top, axis=1)


def shares(amount, total, most, slope, full):
    loads = [(1 << 20) // math.isqrt(standing ** slope) + 1 for standing in range(1, amount + 1)]
    largest = most if full else min(most, max(-(-total // amount), total * loads[0] // sum(loads)))
    least = 1 if total - largest >= amount - 1 else 0
    given, spare = [largest] + [least] * (amount - 1), total - largest - least * (amount - 1)
    while spare > 0:
        movable = [i for i in range(1, amount) if given[i] < largest] or [i for i in range(1, amount) if given[i] < most]
        mass, budget = sum([loads[i] for i in movable]), spare
        for i in movable:
            more = min(most - given[i], max(1, budget * loads[i] // mass), spare)
            given[i] = given[i] + more
            spare = spare - more
    return np.array(given)


def noise(rng, dims, scale, most, shards=(), held_as=jnp.bfloat16):
    drawn = jax.random.normal(rng, dims, jnp.float32) * scale
    if len(shards) > 0:
        drawn = shard_levels(rng, dims, shards, -0.22, 0.18) * drawn
    return jnp.clip(drawn, min=-most, max=most).astype(held_as)


def setup_inputs(seed: int = 0) -> dict:
    streams_of = jax.random.split(jax.random.key(seed), 4)
    centroid = jnp.clip(1.0 * jax.random.uniform(streams_of[0], (3, MOLS), jnp.float32) ** shard_levels(streams_of[0], (3, MOLS), ((1, 32),), -0.2, 0.2), 0.0, 1.0)
    bead_offsets = noise(streams_of[1], (BEADS, 3, MOLS), 0.1, 0.6, ((0, 4), (2, 32)), jnp.float32)
    routes_keys = jax.random.split(jax.random.fold_in(streams_of[2], 1), MOLS // M_DEV)
    routes_turns = jax.random.permutation(jax.random.fold_in(streams_of[2], 3), MOLS // M_DEV)
    routes = jax.vmap(lambda own, number: shared_out(jax.random.fold_in(streams_of[2], 2), own, number, M_DEV, N_SPACE, 1, CAP, 2))(routes_keys, routes_turns).reshape((MOLS, 1))
    return {"centroid": centroid, "bead_offsets": bead_offsets, "routes": routes}


PAIR_SCALE = 0.1
BLOCK_ROWS = 512
REACH_SQUARED = 4.0
BODY_SCALE = 0.1
SLAB_SIDE = 1.5


def contract_table(beads, contracted):
    bead_pos = jnp.arange(beads).astype(jnp.float32)
    coarse = jnp.arange(contracted).astype(jnp.float32)
    phase = 2.0 * math.pi * (bead_pos[None, :] / beads - coarse[:, None] / contracted)
    return (1.0 + 2.0 * jnp.cos(phase)) / beads


def pair_terms(own, other):
    delta = own[:, :, None] - other[:, None, :]
    dist_sq = jnp.sum(delta * delta, axis=0)
    soft = jnp.maximum(1.0 - dist_sq, 0.0)
    weight = 6.0 * PAIR_SCALE * soft * soft
    pushed = weight[None] * delta
    return jnp.sum(pushed, axis=2), -jnp.sum(pushed, axis=1)


def blocked_pairs(own, other):
    rows = own.shape[1]
    block = min(BLOCK_ROWS, rows)
    pieces = own.reshape(3, rows // block, block).transpose(1, 0, 2)

    def step(carry, piece):
        f_own, f_other = pair_terms(piece, other)
        return carry + f_other, f_own

    react, parts = lax.scan(step, jnp.zeros((3, other.shape[1]), jnp.float32), pieces)
    return parts.transpose(1, 0, 2).reshape(3, rows), react


def many_body(pos, valid):
    slots = pos.shape[1]
    block = min(BLOCK_ROWS, slots)
    count = slots // block
    pieces = pos.reshape(3, count, block).transpose(1, 0, 2)
    vpieces = valid.reshape(count, block)

    def weights(piece, vpiece):
        delta = piece[:, :, None] - pos[:, None, :]
        dist_sq = jnp.sum(delta * delta, axis=0)
        near = jnp.maximum(1.0 - dist_sq / REACH_SQUARED, 0.0)
        return delta, vpiece[:, None] * valid[None, :] * near * near

    density = lax.map(lambda item: jnp.sum(weights(item[0], item[1])[1], axis=1), (pieces, vpieces)).reshape(slots)

    def force(item):
        piece, vpiece, rpiece = item
        delta, wgt = weights(piece, vpiece)
        coef = BODY_SCALE * (rpiece[:, None] + density[None, :]) * wgt * wgt
        return jnp.sum(coef[None] * delta, axis=2)

    parts = lax.map(force, (pieces, vpieces, density.reshape(count, block)))
    return parts.transpose(1, 0, 2).reshape(3, slots)


def reference(centroid, bead_offsets, routes):
    scale_vec = jnp.array([1.0, SLAB_SIDE, SLAB_SIDE], jnp.float32)
    unit_x = jnp.array([1.0, 0.0, 0.0], jnp.float32)
    q = scale_vec[None, :, None] * centroid[None] + bead_offsets
    grid = q.reshape(BEADS, 3, N_SPACE, M_DEV)
    left = jnp.roll(grid, 1, axis=2) - unit_x[None, :, None, None]
    right = jnp.roll(grid, -1, axis=2) + unit_x[None, :, None, None]
    others = jnp.concatenate([left, grid, right], axis=3)
    own_t = grid.transpose(0, 2, 1, 3).reshape(BEADS * N_SPACE, 3, M_DEV)
    oth_t = others.transpose(0, 2, 1, 3).reshape(BEADS * N_SPACE, 3, 3 * M_DEV)
    pair2 = lax.map(lambda item: blocked_pairs(item[0], item[1])[0], (own_t, oth_t))
    pair2 = pair2.reshape(BEADS, N_SPACE, 3, M_DEV).transpose(0, 2, 1, 3).reshape(BEADS, 3, MOLS)

    contract = contract_table(BEADS, CONTRACTED)
    slab = (jnp.arange(MOLS) // M_DEV).astype(jnp.float32)
    qc = jnp.einsum("kb,bcm->kcm", contract, q, precision=lax.Precision.HIGHEST)
    qc = qc + unit_x[None, :, None] * slab[None, None, :]

    route = routes[:, 0]
    order = jnp.argsort(route, stable=True).astype(jnp.int32)
    counts = jnp.sum((route[:, None] == jnp.arange(N_SPACE)[None, :]).astype(jnp.int32), axis=0)
    starts = jnp.cumsum(counts) - counts
    place = jnp.arange(SLOTS).astype(jnp.int32)

    def per_domain(acc, dom):
        valid = (place < counts[dom]).astype(jnp.float32)
        members = order[jnp.minimum(starts[dom] + place, MOLS - 1)]
        pos = qc[:, :, members] * valid[None, None, :]
        part = lax.map(lambda p: many_body(p, valid), pos) * valid[None, None, :]
        return acc.at[:, :, members].add(part), None

    many, _ = lax.scan(per_domain, jnp.zeros((CONTRACTED, 3, MOLS), jnp.float32), jnp.arange(N_SPACE).astype(jnp.int32))
    expand = contract.T * (BEADS / CONTRACTED)
    spread = jnp.einsum("bk,kcm->bcm", expand, many, precision=lax.Precision.HIGHEST)
    return pair2 + spread
```

```python
import functools
import math

import jax
import jax.numpy as jnp
import numpy as np
from jax import lax
from jax.experimental import pallas as pl
from jax.experimental.pallas import tpu as pltpu
from jax.sharding import PartitionSpec as P

BEADS = 32
CONTRACTED = 4
PAIR_SCALE = 0.1
BODY_SCALE = 0.1
SLAB_SIDE = 1.5
BAND = 4
FAR = 64.0

f32, bf16 = jnp.float32, jnp.bfloat16
VMEM = pltpu.VMEM


def contract_table():
    phase = 2.0 * math.pi * (np.arange(BEADS)[None, :] / BEADS - np.arange(CONTRACTED)[:, None] / CONTRACTED)
    return ((1.0 + 2.0 * np.cos(phase)) / BEADS).astype(np.float32)


def passed_along(value, axis, by):
    peers = lax.axis_size(axis)
    return lax.ppermute(value, axis, [(i, (i + by) % peers) for i in range(peers)])


def thirds(x):
    high = x.astype(bf16).astype(f32)
    rest = x - high
    mid = rest.astype(bf16).astype(f32)
    return high, mid, rest - mid


def factors(p, reach_sq):
    unit = 1.0 / reach_sq
    high, mid, low = thirds(p)
    norm = 0.5 - unit * jnp.sum(p * p, axis=0, keepdims=True)
    nh, nm, nl = thirds(norm)
    one = jnp.ones_like(norm)
    two = 2.0 * unit
    pad = jnp.zeros((2, p.shape[1]), f32)
    left = [two * high, two * high, two * mid, two * mid, two * high, two * low, two * mid, two * low]
    right = [high, mid, high, mid, low, high, low, mid]
    left = jnp.concatenate(left + [nh, nm, nl, one, one, one, pad], axis=0)
    right = jnp.concatenate(right + [one, one, one, nh, nm, nl, pad], axis=0)
    return left, right


def centre(shift):
    row = lax.broadcasted_iota(jnp.int32, (3, 1), 0)
    return jnp.where(row == 0, 0.5 + shift, 0.5 * SLAB_SIDE).astype(f32)


PAIR_ROWS = 256
PAIR_LANES = 1024


def pair_kernel(shifts, adds, *refs):
    own_ref = refs[0]
    other_refs = refs[1 : 1 + len(shifts)]
    base_ref = refs[1 + len(shifts)] if adds else None
    out_ref, left_s, right_s, terms_s, weight_s, acc_s = refs[-6:]
    mols = own_ref.shape[-1]
    own = own_ref[0] - centre(0.0)
    _, right = factors(own, 1.0)
    right_s[...] = right.astype(bf16)
    acc_s[...] = jnp.zeros_like(acc_s)
    rows = PAIR_ROWS
    steps = mols // rows
    for ref, shift in zip(other_refs, shifts):
        other = ref[0] - centre(-shift)
        left, _ = factors(other, 1.0)
        left_s[...] = left.T.astype(bf16)
        one = jnp.ones((1, mols), f32)
        terms_s[...] = jnp.concatenate([one, *thirds(other), jnp.zeros((6, mols), f32)], axis=0).astype(bf16)

        def weigh(step, slot):
            at = pl.ds(pl.multiple_of(step * rows, rows), rows)
            for lo in range(0, mols, PAIR_LANES):
                lanes = slice(lo, lo + PAIR_LANES)
                soft = jnp.dot(left_s[at, :], right_s[:, lanes], preferred_element_type=f32)
                soft = jnp.maximum(soft, 0.0)
                weight_s[slot, :, lanes] = (soft * soft).astype(bf16)

        def push(step, slot):
            at = pl.ds(pl.multiple_of(step * rows, rows), rows)
            acc_s[...] += jnp.dot(terms_s[:, at], weight_s[slot], preferred_element_type=f32)

        weigh(0, 0)

        def two_steps(turn, carry):
            step = 2 * turn
            weigh(step + 1, 1)
            push(step, 0)
            weigh(jnp.minimum(step + 2, steps - 1), 0)
            push(step + 1, 1)
            return carry

        lax.fori_loop(0, steps // 2, two_steps, 0)
    total = acc_s[...]
    moved = total[1:4] + total[4:7] + total[7:10]
    force = (own * total[0:1] - moved) * f32(6.0 * PAIR_SCALE)
    out_ref[0] = force + base_ref[0] if adds else force


def pair_forces(own, others, shifts, base, first, count):
    mols = own.shape[-1]
    block = pl.BlockSpec((1, 3, mols), lambda b: (b + first if first else b, 0, 0))
    out_block = pl.BlockSpec((1, 3, mols), lambda b: (b, 0, 0))
    arrays = [own, *others]
    specs = [block] * len(arrays)
    if base is not None:
        arrays.append(base)
        specs.append(out_block)
    pairs = count * mols * mols * len(others)
    return pl.pallas_call(
        functools.partial(pair_kernel, shifts, base is not None),
        grid=(count,),
        out_shape=jax.ShapeDtypeStruct((count, 3, mols), f32),
        in_specs=specs,
        out_specs=out_block,
        scratch_shapes=[
            VMEM((mols, 32), bf16),
            VMEM((32, mols), bf16),
            VMEM((16, mols), bf16),
            VMEM((2, PAIR_ROWS, mols), bf16),
            VMEM((16, mols), f32),
        ],
        compiler_params=pltpu.CompilerParams(vmem_limit_bytes=24 << 20),
        cost_estimate=pl.CostEstimate(flops=600 * pairs, bytes_accessed=count * mols * 64, transcendentals=0),
    )(*arrays)


def named(route, domains):
    return (lax.broadcasted_iota(jnp.int32, (domains, route.shape[1]), 0) == route).astype(f32)


def chosen(slot, capacity):
    return (lax.broadcasted_iota(jnp.int32, (capacity, slot.shape[1]), 0) == slot).astype(bf16)


def route_kernel(capacity, pos_ref, route_ref, out_ref, slot_ref, rows_s):
    mols = pos_ref.shape[-1]
    domains = out_ref.shape[0]
    mine = named(route_ref[...], domains)
    width = 128
    up_to = (
        lax.broadcasted_iota(jnp.int32, (width, width), 0) <= lax.broadcasted_iota(jnp.int32, (width, width), 1)
    ).astype(bf16)
    before = jnp.zeros((domains, 1), f32)
    slots = []
    for lo in range(0, mols, width):
        piece = mine[:, lo : lo + width]
        rank = jnp.dot(piece.astype(bf16), up_to, preferred_element_type=f32)
        slots.append(jnp.sum(piece * (rank + before - 1.0), axis=0, keepdims=True))
        before = before + jnp.sum(piece, axis=1, keepdims=True)
    slot = jnp.concatenate(slots, axis=1).astype(jnp.int32)
    slot_ref[...] = slot
    at_slot = chosen(slot, capacity)
    for part, value in enumerate(thirds(pos_ref[...])):
        for c in range(3):
            row = 3 * part + c
            rows_s[row * domains : (row + 1) * domains, :] = (mine * value[c : c + 1]).astype(bf16)
    rows_s[9 * domains :, :] = mine.astype(bf16)
    sent = lax.dot_general(rows_s[...], at_slot, (((1,), (1,)), ((), ())), preferred_element_type=f32)
    sent = sent.reshape(10, domains, capacity)
    for c in range(3):
        value = sent[c] + sent[3 + c] + sent[6 + c]
        if c == 1:
            value = value + FAR * (1.0 - sent[9])
        out_ref[:, c, :] = value
    out_ref[:, 3, :] = sent[9]


def routed(pos, route, domains, capacity):
    mols = pos.shape[-1]
    return pl.pallas_call(
        functools.partial(route_kernel, capacity),
        out_shape=(jax.ShapeDtypeStruct((domains, 4, capacity), f32), jax.ShapeDtypeStruct((1, mols), jnp.int32)),
        in_specs=[pl.BlockSpec(memory_space=VMEM)] * 2,
        out_specs=(pl.BlockSpec(memory_space=VMEM),) * 2,
        scratch_shapes=[VMEM((10 * domains, mols), bf16)],
        compiler_params=pltpu.CompilerParams(vmem_limit_bytes=24 << 20),
        cost_estimate=pl.CostEstimate(flops=1 << 30, bytes_accessed=1 << 18, transcendentals=0),
    )(pos, route)


def unroute_kernel(capacity, back_ref, route_ref, slot_ref, out_ref):
    domains = back_ref.shape[0]
    mine = named(route_ref[...], domains)
    at_slot = chosen(slot_ref[...], capacity)
    for c in range(3):
        rows = jnp.concatenate(thirds(back_ref[:, c, :]), axis=0).astype(bf16)
        spread = jnp.dot(rows, at_slot, preferred_element_type=f32)
        value = spread[:domains] + spread[domains : 2 * domains] + spread[2 * domains :]
        out_ref[c : c + 1, :] = jnp.sum(value * mine, axis=0, keepdims=True)


def unrouted(back, route, slot):
    mols = route.shape[-1]
    return pl.pallas_call(
        functools.partial(unroute_kernel, back.shape[-1]),
        out_shape=jax.ShapeDtypeStruct((3, mols), f32),
        in_specs=[pl.BlockSpec(memory_space=VMEM)] * 3,
        out_specs=pl.BlockSpec(memory_space=VMEM),
        compiler_params=pltpu.CompilerParams(vmem_limit_bytes=24 << 20),
        cost_estimate=pl.CostEstimate(flops=1 << 29, bytes_accessed=1 << 18, transcendentals=0),
    )(back, route, slot)


def body_kernel(slabs, in_ref, out_ref, pos_s, left_s, right_s, terms_s, weight_s, rho_s):
    capacity = in_ref.shape[-1]
    wide = 2 * capacity
    span = min(slabs, 2 * BAND + 2)
    mid = 0.5 * slabs
    for s in range(slabs):
        shift = jnp.where(lax.broadcasted_iota(jnp.int32, (3, 1), 0) == 0, s - mid, -0.5 * SLAB_SIDE)
        pos_s[:, s * capacity : (s + 1) * capacity] = in_ref[s, 0:3, :] + shift.astype(f32)
    pos = pos_s[...]
    left, right = factors(pos, 4.0)
    left_s[...] = left.T.astype(bf16)
    right_s[...] = right.astype(bf16)

    def start_of(tile):
        return jnp.clip(2 * tile - BAND, 0, slabs - span)

    def weigh(tile, carry):
        lanes = pl.ds(pl.multiple_of(tile * wide, wide), wide)
        at = pl.ds(pl.multiple_of(start_of(tile) * capacity, capacity), span * capacity)
        near = jnp.dot(left_s[at, :], right_s[:, lanes], preferred_element_type=f32)
        near = jnp.maximum(near, 0.0)
        weight = near * near
        rho_s[:, lanes] = jnp.sum(weight, axis=0, keepdims=True)
        weight_s[tile] = (weight * weight).astype(bf16)
        return carry

    lax.fori_loop(0, slabs // 2, weigh, 0, unroll=2)
    rho = rho_s[...]
    one = jnp.ones_like(rho)
    blank = jnp.zeros((8, pos.shape[1]), f32)
    terms_s[...] = jnp.concatenate(
        [one, *thirds(pos), *thirds(rho), *thirds(rho * pos), blank, one], axis=0
    ).astype(bf16)

    def push(tile, carry):
        lanes = pl.ds(pl.multiple_of(tile * wide, wide), wide)
        at = pl.ds(pl.multiple_of(start_of(tile) * capacity, capacity), span * capacity)
        total = jnp.dot(terms_s[:, at], weight_s[tile], preferred_element_type=f32)
        here = pos_s[:, lanes]
        plain = here * total[0:1] - (total[1:4] + total[4:7] + total[7:10])
        dense = here * (total[10:11] + total[11:12] + total[12:13]) - (total[13:16] + total[16:19] + total[19:22])
        force = f32(BODY_SCALE) * (rho_s[:, lanes] * plain + dense)
        out_ref[2 * tile, 0:3, :] = force[:, :capacity]
        out_ref[2 * tile + 1, 0:3, :] = force[:, capacity:]
        return carry

    lax.fori_loop(0, slabs // 2, push, 0, unroll=2)
    out_ref[:, 3, :] = jnp.zeros((slabs, capacity), f32)


def body_forces(inbox):
    slabs, _, capacity = inbox.shape
    total = slabs * capacity
    span = min(slabs, 2 * BAND + 2)
    return pl.pallas_call(
        functools.partial(body_kernel, slabs),
        out_shape=jax.ShapeDtypeStruct((slabs, 4, capacity), f32),
        in_specs=[pl.BlockSpec(memory_space=VMEM)],
        out_specs=pl.BlockSpec(memory_space=VMEM),
        scratch_shapes=[
            VMEM((3, total), f32),
            VMEM((total, 32), bf16),
            VMEM((32, total), bf16),
            VMEM((31, total), bf16),
            VMEM((slabs // 2, span * capacity, 2 * capacity), bf16),
            VMEM((1, total), f32),
        ],
        compiler_params=pltpu.CompilerParams(vmem_limit_bytes=32 << 20),
        cost_estimate=pl.CostEstimate(flops=1 << 32, bytes_accessed=1 << 18, transcendentals=0),
    )(inbox)


def shards(centroid, bead_offsets, routes):
    beads_dev, _, mols = bead_offsets.shape
    domains = lax.axis_size("space")
    capacity = 2 * mols // domains
    scale = np.array([1.0, SLAB_SIDE, SLAB_SIDE], np.float32)
    q = scale[None, :, None] * centroid[None] + bead_offsets
    nxt = passed_along(q, "space", -1)
    prev = passed_along(q, "space", 1)

    table = jnp.asarray(contract_table())
    first = lax.axis_index("bead") * beads_dev
    local = lax.dynamic_slice_in_dim(table, first, beads_dev, 1)
    partial = jnp.einsum("kb,bcm->kcm", local, q, precision=lax.Precision.HIGHEST)
    arrived = lax.all_to_all(partial, "bead", split_axis=0, concat_axis=0, tiled=True)
    coarse = arrived.sum(axis=0)
    route = routes.reshape(1, mols)
    outbox, slot = routed(coarse, route, domains, capacity)
    inbox = lax.all_to_all(outbox, "space", split_axis=0, concat_axis=0, tiled=True)
    back = lax.all_to_all(body_forces(inbox), "space", split_axis=0, concat_axis=0, tiled=True)
    mine = unrouted(back, route, slot)
    copies = jnp.broadcast_to(mine, (CONTRACTED, *mine.shape))
    every = lax.all_to_all(copies, "bead", split_axis=0, concat_axis=0, tiled=True)

    own = pair_forces(q, [q], (0.0,), None, 0, beads_dev)
    pair2 = pair_forces(q, [prev, nxt], (-1.0, 1.0), own, 0, beads_dev)
    expand = local.T * (BEADS / CONTRACTED)
    spread = jnp.einsum("bk,kcm->bcm", expand, every, precision=lax.Precision.HIGHEST)
    return pair2 + spread


def solution(mesh):
    placed = (P(None, "space"), P("bead", None, "space"), P("space", None))
    return jax.shard_map(
        shards, mesh=mesh, in_specs=placed, out_specs=P("bead", None, "space"), check_vma=False
    )
```

```python
import functools
import math

import jax
import jax.numpy as jnp
import numpy as np
from jax import lax
from jax.experimental import pallas as pl
from jax.experimental.pallas import tpu as pltpu
from jax.sharding import PartitionSpec as P

BEADS = 32
CONTRACTED = 4
PAIR_SCALE = 0.1
BODY_SCALE = 0.1
SLAB_SIDE = 1.5
BAND = 4
FAR = 64.0


f32, bf16 = jnp.float32, jnp.bfloat16
VMEM = pltpu.VMEM


def contract_table():
    phase = 2.0 * math.pi * (np.arange(BEADS)[None, :] / BEADS - np.arange(CONTRACTED)[:, None] / CONTRACTED)
    return ((1.0 + 2.0 * np.cos(phase)) / BEADS).astype(np.float32)


def passed_along(value, axis, by):
    peers = lax.axis_size(axis)
    return lax.ppermute(value, axis, [(i, (i + by) % peers) for i in range(peers)])


def thirds(x):
    high = x.astype(bf16).astype(f32)
    rest = x - high
    mid = rest.astype(bf16).astype(f32)
    return high, mid, rest - mid


def factors(p, reach_sq):
    unit = 1.0 / reach_sq
    high, mid, low = thirds(p)
    norm = 0.5 - unit * jnp.sum(p * p, axis=0, keepdims=True)
    nh, nm, nl = thirds(norm)
    one = jnp.ones_like(norm)
    two = 2.0 * unit
    pad = jnp.zeros((2, p.shape[1]), f32)
    left = [two * high, two * high, two * mid, two * mid, two * high, two * low, two * mid, two * low]
    right = [high, mid, high, mid, low, high, low, mid]
    left = jnp.concatenate(left + [nh, nm, nl, one, one, one, pad], axis=0)
    right = jnp.concatenate(right + [one, one, one, nh, nm, nl, pad], axis=0)
    return left, right


SIDE = 256
LANES = 128


def centred(ref, bead, shift):
    mols = ref.shape[-1]
    mids = (0.5 - shift, 0.5 * SLAB_SIDE, 0.5 * SLAB_SIDE)
    q = jnp.concatenate([ref[c, pl.ds(bead, 1), :] - f32(mids[c]) for c in range(3)], axis=0)
    norm = 0.5 - jnp.sum(q * q, axis=0, keepdims=True)
    return jnp.concatenate([q, norm, jnp.ones((1, mols), f32), jnp.zeros((3, mols), f32)], axis=0)


def pair_left(p):
    row = lax.broadcasted_iota(jnp.int32, p.shape, 0)
    high, mid, low = thirds(p)
    place, norm, one = row < 3, row == 3, row == 4
    blocks = [
        high,
        jnp.where(norm, mid, high),
        jnp.where(norm, low, jnp.where(one, 1.0, mid)),
        jnp.where(place, mid, 0.0),
        jnp.where(place, high, 0.0),
        jnp.where(place, low, 0.0),
    ]
    return jnp.concatenate(blocks, axis=0)


def pair_right(p):
    row = lax.broadcasted_iota(jnp.int32, p.shape, 0)
    high, mid, low = thirds(p)
    place, norm, one = row < 3, row == 3, row == 4

    def both(x, part):
        rest = jnp.where(norm, 1.0, jnp.where(one, part[3:4], 0.0))
        return jnp.where(place, 2.0 * x, rest)

    def alone(x):
        return jnp.where(place, 2.0 * x, 0.0)

    blocks = [both(high, high), both(mid, mid), both(high, low), alone(mid), alone(low), alone(high)]
    return jnp.concatenate(blocks, axis=0)


def pair_terms(p):
    row = lax.broadcasted_iota(jnp.int32, p.shape, 0)
    high, mid, _ = thirds(p)
    return jnp.concatenate([high, jnp.where(row < 3, mid, 0.0)], axis=0).astype(bf16)


def put_left(left_s, p):
    rows = jnp.concatenate([pair_left(p), jnp.zeros((16, p.shape[1]), f32)], axis=0)
    left_s[...] = rows.T.astype(bf16)


def weigh(left_s, right_s, weight_s, slot, block, lane, count):
    at = pl.ds(pl.multiple_of(block * SIDE, SIDE), SIDE)
    lanes = slice(lane * LANES, (lane + count) * LANES)
    soft = jnp.dot(left_s[at, 0:48], right_s[:, lanes], preferred_element_type=f32)
    soft = jnp.maximum(soft, 0.0)
    weight = (soft * soft).astype(bf16)
    for k in range(count):
        weight_s[slot, lane + k] = weight[:, k * LANES : (k + 1) * LANES]


def turn(weight_s, turned_s, slot, lane):
    turned = weight_s[slot, lane].T
    for k in range(SIDE // LANES):
        turned_s[slot, k, lane * LANES : (lane + 1) * LANES, :] = turned[:, k * LANES : (k + 1) * LANES]


def wide(ref, slot, lane, rows=slice(None)):
    return jnp.concatenate([ref[slot, lane, rows, :], ref[slot, lane + 1, rows, :]], axis=1)


def force_of(p, acc):
    return (p[0:3] * acc[4:5] - (acc[0:3] + acc[8:11])) * f32(6.0 * PAIR_SCALE)


def add_rows(out_ref, bead, force):
    for c in range(3):
        out_ref[c, pl.ds(bead, 1), :] += force[c : c + 1]


def cross_kernel(first, n_after, own_ref, next_ref, *refs):
    base_ref, react_in_ref = refs[0:2]
    out_ref, react_ref = refs[2 + n_after : 4 + n_after]
    left_s, right_s, own_s, next_s, weight_s, turned_s, acc_s, react_s = refs[4 + n_after :]
    mols = own_ref.shape[-1]

    @pl.when(pl.program_id(0) == 0)
    def _():
        out_ref[...] = base_ref[...]
        react_ref[...] = react_in_ref[...]

    bead = pl.program_id(0) + first
    own, nxt = centred(own_ref, bead, 0.0), centred(next_ref, bead, 1.0)
    right_s[...] = pair_right(own).astype(bf16)
    put_left(left_s, nxt)
    own_s[...], next_s[...] = pair_terms(own), pair_terms(nxt)
    tiles, steps = mols // LANES, mols // SIDE
    group = min(8, tiles)

    def fill(step, slot):
        for lane in range(0, tiles, group):
            weigh(left_s, right_s, weight_s, slot, step, lane, group)

    def push(step, slot, fresh=False):
        terms = next_s[:, pl.ds(pl.multiple_of(step * SIDE, SIDE), SIDE)]
        for lane in range(0, tiles, 2):
            part = jnp.dot(terms, wide(weight_s, slot, lane), preferred_element_type=f32)
            lanes = slice(lane * LANES, (lane + 2) * LANES)
            if fresh:
                acc_s[:, lanes] = part
            else:
                acc_s[:, lanes] += part

    def flip(slot):
        for lane in range(tiles):
            turn(weight_s, turned_s, slot, lane)

    def back(step, slot):
        at = pl.ds(pl.multiple_of(step * SIDE, SIDE), SIDE)
        react_s[:, at] = jnp.dot(own_s[...], wide(turned_s, slot, 0), preferred_element_type=f32)

    fill(0, 0)
    fill(1, 1)
    push(0, 0, True)
    flip(0)

    def two_steps(turn_no, carry):
        step = 2 * turn_no + 1
        fill(step + 1, 0)
        push(step, 1)
        flip(1)
        back(step - 1, 0)
        fill(step + 2, 1)
        push(step + 1, 0)
        flip(0)
        back(step, 1)
        return carry

    lax.fori_loop(0, (steps - 2) // 2, two_steps, 0)
    push(steps - 1, 1)
    flip(1)
    back(steps - 2, 0)
    back(steps - 1, 1)
    add_rows(out_ref, bead, force_of(own, acc_s[...]))
    add_rows(react_ref, bead, force_of(nxt, react_s[...]))


def self_kernel(first, n_after, fresh, own_ref, *refs):
    base_ref = None if fresh else refs[0]
    skip = n_after + (0 if fresh else 1)
    out_ref, left_s, right_s, own_s, weight_s, turned_s, acc_s = refs[skip:]
    mols = own_ref.shape[-1]

    @pl.when(pl.program_id(0) == 0)
    def _():
        out_ref[...] = jnp.zeros_like(out_ref) if fresh else base_ref[...]

    bead = pl.program_id(0) + first
    own = centred(own_ref, bead, 0.0)
    right_s[...] = pair_right(own).astype(bf16)
    put_left(left_s, own)
    own_s[...] = pair_terms(own)
    acc_s[...] = jnp.zeros_like(acc_s)
    tiles, steps = mols // LANES, mols // SIDE

    for step in range(steps + 2):
        if step < steps:
            for lane in range(2 * step, tiles, 2):
                weigh(left_s, right_s, weight_s, step % 2, step, lane, 2)
        now = step - 1
        if 0 <= now < steps:
            terms = own_s[:, now * SIDE : (now + 1) * SIDE]
            for lane in range(2 * now, tiles, 2):
                lanes = slice(lane * LANES, (lane + 2) * LANES)
                acc_s[:, lanes] += jnp.dot(terms, wide(weight_s, now % 2, lane), preferred_element_type=f32)
            for lane in range(2 * now + 2, tiles):
                turn(weight_s, turned_s, now % 2, lane)
        now = step - 2
        if 0 <= now < steps - 1:
            rows = slice((now + 1) * SIDE, mols)
            part = jnp.dot(own_s[:, rows], wide(turned_s, now % 2, 0, rows), preferred_element_type=f32)
            acc_s[:, now * SIDE : (now + 1) * SIDE] += part
    add_rows(out_ref, bead, force_of(own, acc_s[...]))


def pair_call(kernel, arrays, after, outs, count, n_terms, n_acc, blocks):
    mols = arrays[0].shape[-1]
    whole = pl.BlockSpec(arrays[0].shape, lambda b: (0, 0, 0))
    shape = jax.ShapeDtypeStruct(arrays[0].shape, f32)
    return pl.pallas_call(
        kernel,
        grid=(count,),
        out_shape=(shape,) * outs,
        in_specs=[whole] * len(arrays) + [pl.BlockSpec(memory_space=pl.ANY)] * len(after),
        out_specs=(whole,) * outs,
        scratch_shapes=[
            VMEM((mols, 64), bf16),
            VMEM((48, mols), bf16),
            *[VMEM((16, mols), bf16)] * n_terms,
            VMEM((2, mols // LANES, SIDE, LANES), bf16),
            VMEM((2, SIDE // LANES, mols, LANES), bf16),
            *[VMEM((16, mols), f32)] * n_acc,
        ],
        compiler_params=pltpu.CompilerParams(vmem_limit_bytes=24 << 20),
        cost_estimate=pl.CostEstimate(flops=count * blocks * (200 << 20), bytes_accessed=1 << 20, transcendentals=0),
    )(*arrays, *after)


def cross_pairs(own, nxt, base, react, first, count, after=()):
    kernel = functools.partial(cross_kernel, first, len(after))
    blocks = (own.shape[-1] // SIDE) ** 2
    return pair_call(kernel, [own, nxt, base, react], after, 2, count, 2, 2, blocks)


def self_pairs(own, base, first, count, after=()):
    kernel = functools.partial(self_kernel, first, len(after), base is None)
    blocks = (own.shape[-1] // SIDE) ** 2 // 2
    arrays = [own] if base is None else [own, base]
    return pair_call(kernel, arrays, after, 1, count, 1, 1, blocks)[0]


def named(route, domains):
    return (lax.broadcasted_iota(jnp.int32, (domains, route.shape[1]), 0) == route).astype(f32)


def chosen(slot, capacity):
    return (lax.broadcasted_iota(jnp.int32, (capacity, slot.shape[1]), 0) == slot).astype(bf16)


def route_kernel(capacity, pos_ref, route_ref, _, out_ref, slot_ref, rows_s):
    mols = pos_ref.shape[-1]
    domains = out_ref.shape[0]
    mine = named(route_ref[...], domains)
    width = 128
    up_to = (
        lax.broadcasted_iota(jnp.int32, (width, width), 0) <= lax.broadcasted_iota(jnp.int32, (width, width), 1)
    ).astype(bf16)
    before = jnp.zeros((domains, 1), f32)
    slots = []
    for lo in range(0, mols, width):
        piece = mine[:, lo : lo + width]
        rank = jnp.dot(piece.astype(bf16), up_to, preferred_element_type=f32)
        slots.append(jnp.sum(piece * (rank + before - 1.0), axis=0, keepdims=True))
        before = before + jnp.sum(piece, axis=1, keepdims=True)
    slot = jnp.concatenate(slots, axis=1).astype(jnp.int32)
    slot_ref[...] = slot
    at_slot = chosen(slot, capacity)
    for part, value in enumerate(thirds(pos_ref[...])):
        for c in range(3):
            row = 3 * part + c
            rows_s[row * domains : (row + 1) * domains, :] = (mine * value[c : c + 1]).astype(bf16)
    rows_s[9 * domains :, :] = mine.astype(bf16)
    sent = lax.dot_general(rows_s[...], at_slot, (((1,), (1,)), ((), ())), preferred_element_type=f32)
    sent = sent.reshape(10, domains, capacity)
    for c in range(3):
        value = sent[c] + sent[3 + c] + sent[6 + c]
        if c == 1:
            value = value + FAR * (1.0 - sent[9])
        out_ref[:, c, :] = value
    out_ref[:, 3, :] = sent[9]


def routed(pos, route, domains, capacity, after):
    mols = pos.shape[-1]
    return pl.pallas_call(
        functools.partial(route_kernel, capacity),
        out_shape=(jax.ShapeDtypeStruct((domains, 4, capacity), f32), jax.ShapeDtypeStruct((1, mols), jnp.int32)),
        in_specs=[pl.BlockSpec(memory_space=VMEM)] * 2 + [pl.BlockSpec(memory_space=pl.ANY)],
        out_specs=(pl.BlockSpec(memory_space=VMEM),) * 2,
        scratch_shapes=[VMEM((10 * domains, mols), bf16)],
        compiler_params=pltpu.CompilerParams(vmem_limit_bytes=24 << 20),
        cost_estimate=pl.CostEstimate(flops=1 << 30, bytes_accessed=1 << 18, transcendentals=0),
    )(pos, route, after)


def unroute_kernel(capacity, back_ref, route_ref, slot_ref, _, out_ref):
    domains = back_ref.shape[0]
    mine = named(route_ref[...], domains)
    at_slot = chosen(slot_ref[...], capacity)
    for c in range(3):
        rows = jnp.concatenate(thirds(back_ref[:, c, :]), axis=0).astype(bf16)
        spread = jnp.dot(rows, at_slot, preferred_element_type=f32)
        value = spread[:domains] + spread[domains : 2 * domains] + spread[2 * domains :]
        out_ref[c : c + 1, :] = jnp.sum(value * mine, axis=0, keepdims=True)


def unrouted(back, route, slot, after):
    mols = route.shape[-1]
    return pl.pallas_call(
        functools.partial(unroute_kernel, back.shape[-1]),
        out_shape=jax.ShapeDtypeStruct((3, mols), f32),
        in_specs=[pl.BlockSpec(memory_space=VMEM)] * 3 + [pl.BlockSpec(memory_space=pl.ANY)],
        out_specs=pl.BlockSpec(memory_space=VMEM),
        compiler_params=pltpu.CompilerParams(vmem_limit_bytes=24 << 20),
        cost_estimate=pl.CostEstimate(flops=1 << 29, bytes_accessed=1 << 18, transcendentals=0),
    )(back, route, slot, after)


def body_kernel(slabs, in_ref, _, out_ref, pos_s, left_s, right_s, terms_s, weight_s, rho_s):
    capacity = in_ref.shape[-1]
    wide = 2 * capacity
    span = min(slabs, 2 * BAND + 2)
    mid = 0.5 * slabs
    for s in range(slabs):
        shift = jnp.where(lax.broadcasted_iota(jnp.int32, (3, 1), 0) == 0, s - mid, -0.5 * SLAB_SIDE)
        pos_s[:, s * capacity : (s + 1) * capacity] = in_ref[s, 0:3, :] + shift.astype(f32)
    pos = pos_s[...]
    left, right = factors(pos, 4.0)
    left_s[...] = left.T.astype(bf16)
    right_s[...] = right.astype(bf16)

    def start_of(tile):
        return jnp.clip(2 * tile - BAND, 0, slabs - span)

    def weigh(tile, carry):
        lanes = pl.ds(pl.multiple_of(tile * wide, wide), wide)
        at = pl.ds(pl.multiple_of(start_of(tile) * capacity, capacity), span * capacity)
        near = jnp.dot(left_s[at, :], right_s[:, lanes], preferred_element_type=f32)
        near = jnp.maximum(near, 0.0)
        weight = near * near
        rho_s[:, lanes] = jnp.sum(weight, axis=0, keepdims=True)
        weight_s[tile] = (weight * weight).astype(bf16)
        return carry

    lax.fori_loop(0, slabs // 2, weigh, 0, unroll=2)
    rho = rho_s[...]
    one = jnp.ones_like(rho)
    blank = jnp.zeros((8, pos.shape[1]), f32)
    terms_s[...] = jnp.concatenate(
        [one, *thirds(pos), *thirds(rho), *thirds(rho * pos), blank, one], axis=0
    ).astype(bf16)

    def push(tile, carry):
        lanes = pl.ds(pl.multiple_of(tile * wide, wide), wide)
        at = pl.ds(pl.multiple_of(start_of(tile) * capacity, capacity), span * capacity)
        total = jnp.dot(terms_s[:, at], weight_s[tile], preferred_element_type=f32)
        here = pos_s[:, lanes]
        plain = here * total[0:1] - (total[1:4] + total[4:7] + total[7:10])
        dense = here * (total[10:11] + total[11:12] + total[12:13]) - (total[13:16] + total[16:19] + total[19:22])
        force = f32(BODY_SCALE) * (rho_s[:, lanes] * plain + dense)
        out_ref[2 * tile, 0:3, :] = force[:, :capacity]
        out_ref[2 * tile + 1, 0:3, :] = force[:, capacity:]
        return carry

    lax.fori_loop(0, slabs // 2, push, 0, unroll=2)
    out_ref[:, 3, :] = jnp.zeros((slabs, capacity), f32)


def body_forces(inbox, after):
    slabs, _, capacity = inbox.shape
    total = slabs * capacity
    span = min(slabs, 2 * BAND + 2)
    return pl.pallas_call(
        functools.partial(body_kernel, slabs),
        out_shape=jax.ShapeDtypeStruct((slabs, 4, capacity), f32),
        in_specs=[pl.BlockSpec(memory_space=VMEM), pl.BlockSpec(memory_space=pl.ANY)],
        out_specs=pl.BlockSpec(memory_space=VMEM),
        scratch_shapes=[
            VMEM((3, total), f32),
            VMEM((total, 32), bf16),
            VMEM((32, total), bf16),
            VMEM((31, total), bf16),
            VMEM((slabs // 2, span * capacity, 2 * capacity), bf16),
            VMEM((1, total), f32),
        ],
        compiler_params=pltpu.CompilerParams(vmem_limit_bytes=32 << 20),
        cost_estimate=pl.CostEstimate(flops=1 << 32, bytes_accessed=1 << 18, transcendentals=0),
    )(inbox, after)


def shards(centroid, bead_offsets, routes):
    beads_dev, _, mols = bead_offsets.shape
    domains = lax.axis_size("space")
    ring = lax.axis_size("bead")
    capacity = 2 * mols // domains
    half = beads_dev // 2
    scale = np.array([1.0, SLAB_SIDE, SLAB_SIDE], np.float32)
    q = scale[:, None, None] * centroid[:, None, :] + bead_offsets.transpose(1, 0, 2)
    nxt = passed_along(q, "space", -1)

    table = contract_table()
    place = lax.axis_index("bead")
    first = place * beads_dev
    ahead = lax.dynamic_slice(jnp.asarray(np.concatenate([table, table])), (place, first), (ring, beads_dev))
    back = np.roll(table[::-1], 1, axis=0)
    behind = lax.dynamic_slice(jnp.asarray(np.concatenate([back, back])), (ring - place, first), (ring, beads_dev))
    partial = jnp.einsum("kb,cbm->kcm", ahead, q, precision=lax.Precision.HIGHEST)
    coarse = partial[0]
    for by in range(1, ring):
        coarse = coarse + passed_along(partial[by], "bead", by)

    force = self_pairs(q, None, 0, half)
    route = routes.reshape(1, mols)
    outbox, slot = routed(coarse, route, domains, capacity, force)
    inbox = lax.all_to_all(outbox, "space", split_axis=0, concat_axis=0, tiled=True)
    force, react = cross_pairs(q, nxt, force, jnp.zeros_like(q), 0, half, (outbox,))
    bodies = body_forces(inbox, force)
    returned = lax.all_to_all(bodies, "space", split_axis=0, concat_axis=0, tiled=True)
    force, react = cross_pairs(q, nxt, force, react, half, half, (bodies,))
    mine = unrouted(returned, route, slot, force)
    arrived = passed_along(react, "space", 1)
    every = [mine] + [passed_along(mine, "bead", by) for by in range(1, ring)]
    force = self_pairs(q, force, half, half, (mine,))
    total = force + arrived
    for by in range(ring):
        share = behind[by] * f32(BEADS / CONTRACTED)
        total = total + share[None, :, None] * every[by][:, None, :]
    return total.transpose(1, 0, 2)


def solution(mesh):
    placed = (P(None, "space"), P("bead", None, "space"), P("space", None))
    return jax.shard_map(
        shards, mesh=mesh, in_specs=placed, out_specs=P("bead", None, "space"), check_vma=False
    )
```

```python
import functools
import math

import jax
import jax.numpy as jnp
import numpy as np
from jax import lax
from jax.experimental import pallas as pl
from jax.experimental.pallas import tpu as pltpu
from jax.sharding import PartitionSpec as P

BEADS = 32
CONTRACTED = 4
PAIR_SCALE = 0.1
BODY_SCALE = 0.1
SLAB_SIDE = 1.5
BAND = 4
FAR = 64.0


f32, bf16 = jnp.float32, jnp.bfloat16
VMEM = pltpu.VMEM


def contract_table():
    phase = 2.0 * math.pi * (np.arange(BEADS)[None, :] / BEADS - np.arange(CONTRACTED)[:, None] / CONTRACTED)
    return ((1.0 + 2.0 * np.cos(phase)) / BEADS).astype(np.float32)


def passed_along(value, axis, by):
    peers = lax.axis_size(axis)
    return lax.ppermute(value, axis, [(i, (i + by) % peers) for i in range(peers)])


def thirds(x):
    high = x.astype(bf16).astype(f32)
    rest = x - high
    mid = rest.astype(bf16).astype(f32)
    return high, mid, rest - mid


SIDE = 256
LANES = 128


def with_norm(q):
    mols = q.shape[-1]
    norm = 0.5 - jnp.sum(q * q, axis=0, keepdims=True)
    return jnp.concatenate([q, norm, jnp.ones((1, mols), f32), jnp.zeros((3, mols), f32)], axis=0)


def centred(ref, bead, shift):
    mids = (0.5 - shift, 0.5 * SLAB_SIDE, 0.5 * SLAB_SIDE)
    return with_norm(jnp.concatenate([ref[c, pl.ds(bead, 1), :] - f32(mids[c]) for c in range(3)], axis=0))


def pair_left(p):
    row = lax.broadcasted_iota(jnp.int32, p.shape, 0)
    high, mid, low = thirds(p)
    place, norm, one = row < 3, row == 3, row == 4
    blocks = [
        high,
        jnp.where(norm, mid, high),
        jnp.where(norm, low, jnp.where(one, 1.0, mid)),
        jnp.where(place, mid, 0.0),
        jnp.where(place, high, 0.0),
        jnp.where(place, low, 0.0),
    ]
    return jnp.concatenate(blocks, axis=0)


def pair_right(p):
    row = lax.broadcasted_iota(jnp.int32, p.shape, 0)
    high, mid, low = thirds(p)
    place, norm, one = row < 3, row == 3, row == 4

    def both(x, part):
        rest = jnp.where(norm, 1.0, jnp.where(one, part[3:4], 0.0))
        return jnp.where(place, 2.0 * x, rest)

    def alone(x):
        return jnp.where(place, 2.0 * x, 0.0)

    blocks = [both(high, high), both(mid, mid), both(high, low), alone(mid), alone(low), alone(high)]
    return jnp.concatenate(blocks, axis=0)


def pair_terms(p):
    row = lax.broadcasted_iota(jnp.int32, p.shape, 0)
    high, mid, _ = thirds(p)
    return jnp.concatenate([high, jnp.where(row < 3, mid, 0.0)], axis=0).astype(bf16)


def put_left(left_s, p):
    rows = jnp.concatenate([pair_left(p), jnp.zeros((16, p.shape[1]), f32)], axis=0)
    left_s[...] = rows.T.astype(bf16)


def weigh(left_s, right_s, weight_s, slot, block, lane, count):
    at = pl.ds(pl.multiple_of(block * SIDE, SIDE), SIDE)
    lanes = slice(lane * LANES, (lane + count) * LANES)
    soft = jnp.dot(left_s[at, 0:48], right_s[:, lanes], preferred_element_type=f32)
    soft = jnp.maximum(soft, 0.0)
    weight = (soft * soft).astype(bf16)
    for k in range(count):
        weight_s[slot, lane + k] = weight[:, k * LANES : (k + 1) * LANES]


def turn(weight_s, turned_s, slot, lane):
    turned = weight_s[slot, lane].T
    for k in range(SIDE // LANES):
        turned_s[slot, k, lane * LANES : (lane + 1) * LANES, :] = turned[:, k * LANES : (k + 1) * LANES]


def wide(ref, slot, lane, rows=slice(None)):
    return jnp.concatenate([ref[slot, lane, rows, :], ref[slot, lane + 1, rows, :]], axis=1)


def force_of(p, acc):
    return (p[0:3] * acc[4:5] - (acc[0:3] + acc[8:11])) * f32(6.0 * PAIR_SCALE)


def add_rows(out_ref, bead, force):
    for c in range(3):
        out_ref[c, pl.ds(bead, 1), :] += force[c : c + 1]


def cross_kernel(first, n_after, own_ref, next_ref, *refs):
    base_ref, react_in_ref = refs[0:2]
    out_ref, react_ref = refs[2 + n_after : 4 + n_after]
    left_s, right_s, own_s, next_s, weight_s, turned_s, acc_s, react_s = refs[4 + n_after :]
    mols = own_ref.shape[-1]

    @pl.when(pl.program_id(0) == 0)
    def _():
        out_ref[...] = base_ref[...]
        react_ref[...] = react_in_ref[...]

    bead = pl.program_id(0) + first
    own, nxt = centred(own_ref, bead, 0.0), centred(next_ref, bead, 1.0)
    right_s[...] = pair_right(own).astype(bf16)
    put_left(left_s, nxt)
    own_s[...], next_s[...] = pair_terms(own), pair_terms(nxt)
    tiles, steps = mols // LANES, mols // SIDE
    group = min(8, tiles)

    def fill(step, slot):
        for lane in range(0, tiles, group):
            weigh(left_s, right_s, weight_s, slot, step, lane, group)

    def push(step, slot, fresh=False):
        terms = next_s[:, pl.ds(pl.multiple_of(step * SIDE, SIDE), SIDE)]
        for lane in range(0, tiles, 2):
            part = jnp.dot(terms, wide(weight_s, slot, lane), preferred_element_type=f32)
            lanes = slice(lane * LANES, (lane + 2) * LANES)
            if fresh:
                acc_s[:, lanes] = part
            else:
                acc_s[:, lanes] += part

    def flip(slot):
        for lane in range(tiles):
            turn(weight_s, turned_s, slot, lane)

    def back(step, slot):
        at = pl.ds(pl.multiple_of(step * SIDE, SIDE), SIDE)
        react_s[:, at] = jnp.dot(own_s[...], wide(turned_s, slot, 0), preferred_element_type=f32)

    fill(0, 0)
    fill(1, 1)
    push(0, 0, True)
    flip(0)

    def two_steps(turn_no, carry):
        step = 2 * turn_no + 1
        fill(step + 1, 0)
        push(step, 1)
        flip(1)
        back(step - 1, 0)
        fill(step + 2, 1)
        push(step + 1, 0)
        flip(0)
        back(step, 1)
        return carry

    lax.fori_loop(0, (steps - 2) // 2, two_steps, 0)
    push(steps - 1, 1)
    flip(1)
    back(steps - 2, 0)
    back(steps - 1, 1)
    add_rows(out_ref, bead, force_of(own, acc_s[...]))
    add_rows(react_ref, bead, force_of(nxt, react_s[...]))


def self_kernel(first, n_after, fresh, own_ref, *refs):
    base_ref = None if fresh else refs[0]
    skip = n_after + (0 if fresh else 1)
    out_ref, left_s, right_s, own_s, weight_s, turned_s, acc_s = refs[skip:]
    mols = own_ref.shape[-1]

    @pl.when(pl.program_id(0) == 0)
    def _():
        out_ref[...] = jnp.zeros_like(out_ref) if fresh else base_ref[...]

    bead = pl.program_id(0) + first
    own = centred(own_ref, bead, 0.0)
    right_s[...] = pair_right(own).astype(bf16)
    put_left(left_s, own)
    own_s[...] = pair_terms(own)
    acc_s[...] = jnp.zeros_like(acc_s)
    tiles, steps = mols // LANES, mols // SIDE

    for step in range(steps + 2):
        if step < steps:
            for lane in range(2 * step, tiles, 2):
                weigh(left_s, right_s, weight_s, step % 2, step, lane, 2)
        now = step - 1
        if 0 <= now < steps:
            terms = own_s[:, now * SIDE : (now + 1) * SIDE]
            for lane in range(2 * now, tiles, 2):
                lanes = slice(lane * LANES, (lane + 2) * LANES)
                acc_s[:, lanes] += jnp.dot(terms, wide(weight_s, now % 2, lane), preferred_element_type=f32)
            for lane in range(2 * now + 2, tiles):
                turn(weight_s, turned_s, now % 2, lane)
        now = step - 2
        if 0 <= now < steps - 1:
            rows = slice((now + 1) * SIDE, mols)
            part = jnp.dot(own_s[:, rows], wide(turned_s, now % 2, 0, rows), preferred_element_type=f32)
            acc_s[:, now * SIDE : (now + 1) * SIDE] += part
    add_rows(out_ref, bead, force_of(own, acc_s[...]))


def pair_call(kernel, arrays, after, outs, count, n_terms, n_acc, blocks):
    mols = arrays[0].shape[-1]
    whole = pl.BlockSpec(arrays[0].shape, lambda b: (0, 0, 0))
    shape = jax.ShapeDtypeStruct(arrays[0].shape, f32)
    return pl.pallas_call(
        kernel,
        grid=(count,),
        out_shape=(shape,) * outs,
        in_specs=[whole] * len(arrays) + [pl.BlockSpec(memory_space=pl.ANY)] * len(after),
        out_specs=(whole,) * outs,
        scratch_shapes=[
            VMEM((mols, 64), bf16),
            VMEM((48, mols), bf16),
            *[VMEM((16, mols), bf16)] * n_terms,
            VMEM((2, mols // LANES, SIDE, LANES), bf16),
            VMEM((2, SIDE // LANES, mols, LANES), bf16),
            *[VMEM((16, mols), f32)] * n_acc,
        ],
        compiler_params=pltpu.CompilerParams(vmem_limit_bytes=24 << 20),
        cost_estimate=pl.CostEstimate(flops=count * blocks * (200 << 20), bytes_accessed=1 << 20, transcendentals=0),
    )(*arrays, *after)


def cross_pairs(own, nxt, base, react, first, count, after=()):
    kernel = functools.partial(cross_kernel, first, len(after))
    blocks = (own.shape[-1] // SIDE) ** 2
    return pair_call(kernel, [own, nxt, base, react], after, 2, count, 2, 2, blocks)


def self_pairs(own, base, first, count, after=()):
    kernel = functools.partial(self_kernel, first, len(after), base is None)
    blocks = (own.shape[-1] // SIDE) ** 2 // 2
    arrays = [own] if base is None else [own, base]
    return pair_call(kernel, arrays, after, 1, count, 1, 1, blocks)[0]


def named(route, domains):
    return (lax.broadcasted_iota(jnp.int32, (domains, route.shape[1]), 0) == route).astype(f32)


def chosen(slot, capacity):
    return (lax.broadcasted_iota(jnp.int32, (capacity, slot.shape[1]), 0) == slot).astype(bf16)


def route_kernel(capacity, *refs):
    *part_refs, route_ref, _, out_ref, slot_ref, rows_s = refs
    pos = sum(ref[...] for ref in part_refs)
    mols = pos.shape[-1]
    domains = out_ref.shape[0]
    mine = named(route_ref[...], domains)
    width = 128
    up_to = (
        lax.broadcasted_iota(jnp.int32, (width, width), 0) <= lax.broadcasted_iota(jnp.int32, (width, width), 1)
    ).astype(bf16)
    before = jnp.zeros((domains, 1), f32)
    slots = []
    for lo in range(0, mols, width):
        piece = mine[:, lo : lo + width]
        rank = jnp.dot(piece.astype(bf16), up_to, preferred_element_type=f32)
        slots.append(jnp.sum(piece * (rank + before - 1.0), axis=0, keepdims=True))
        before = before + jnp.sum(piece, axis=1, keepdims=True)
    slot = jnp.concatenate(slots, axis=1).astype(jnp.int32)
    slot_ref[...] = slot
    at_slot = chosen(slot, capacity)
    for part, value in enumerate(thirds(pos)):
        for c in range(3):
            row = 3 * part + c
            rows_s[row * domains : (row + 1) * domains, :] = (mine * value[c : c + 1]).astype(bf16)
    rows_s[9 * domains :, :] = mine.astype(bf16)
    sent = lax.dot_general(rows_s[...], at_slot, (((1,), (1,)), ((), ())), preferred_element_type=f32)
    sent = sent.reshape(10, domains, capacity)
    for c in range(3):
        value = sent[c] + sent[3 + c] + sent[6 + c]
        if c == 1:
            value = value + FAR * (1.0 - sent[9])
        out_ref[:, c, :] = value
    out_ref[:, 3, :] = sent[9]


def routed(parts, route, domains, capacity, after):
    mols = route.shape[-1]
    return pl.pallas_call(
        functools.partial(route_kernel, capacity),
        out_shape=(jax.ShapeDtypeStruct((domains, 4, capacity), f32), jax.ShapeDtypeStruct((1, mols), jnp.int32)),
        in_specs=[pl.BlockSpec(memory_space=VMEM)] * (len(parts) + 1) + [pl.BlockSpec(memory_space=pl.ANY)],
        out_specs=(pl.BlockSpec(memory_space=VMEM),) * 2,
        scratch_shapes=[VMEM((10 * domains, mols), bf16)],
        compiler_params=pltpu.CompilerParams(vmem_limit_bytes=24 << 20),
        cost_estimate=pl.CostEstimate(flops=1 << 30, bytes_accessed=1 << 18, transcendentals=0),
    )(*parts, route, after)


def unroute_kernel(capacity, back_ref, route_ref, slot_ref, _, out_ref):
    domains = back_ref.shape[0]
    mine = named(route_ref[...], domains)
    at_slot = chosen(slot_ref[...], capacity)
    for c in range(3):
        rows = jnp.concatenate(thirds(back_ref[:, c, :]), axis=0).astype(bf16)
        spread = jnp.dot(rows, at_slot, preferred_element_type=f32)
        value = spread[:domains] + spread[domains : 2 * domains] + spread[2 * domains :]
        out_ref[c : c + 1, :] = jnp.sum(value * mine, axis=0, keepdims=True)


def unrouted(back, route, slot, after):
    mols = route.shape[-1]
    return pl.pallas_call(
        functools.partial(unroute_kernel, back.shape[-1]),
        out_shape=jax.ShapeDtypeStruct((3, mols), f32),
        in_specs=[pl.BlockSpec(memory_space=VMEM)] * 3 + [pl.BlockSpec(memory_space=pl.ANY)],
        out_specs=pl.BlockSpec(memory_space=VMEM),
        compiler_params=pltpu.CompilerParams(vmem_limit_bytes=24 << 20),
        cost_estimate=pl.CostEstimate(flops=1 << 29, bytes_accessed=1 << 18, transcendentals=0),
    )(back, route, slot, after)


def body_kernel(slabs, in_ref, _, out_ref, pos_s, left_s, right_s, terms_s, high_s, low_s, rho_s):
    capacity = in_ref.shape[-1]
    pair = 2 * capacity
    for s in range(slabs):
        pos_s[0:4, s * capacity : (s + 1) * capacity] = in_ref[s]
    lane = lax.broadcasted_iota(jnp.int32, (1, slabs * capacity), 1)
    slab = (lane // capacity).astype(f32) - 0.5 * slabs
    x = 0.5 * (pos_s[0:1, :] + slab)
    yz = 0.5 * (pos_s[1:3, :] - 0.5 * SLAB_SIDE)
    used = pos_s[3:4, :] > 0.5
    pos = with_norm(jnp.concatenate([x, yz], axis=0))
    left = jnp.concatenate([pair_left(pos), jnp.zeros((16, pos.shape[1]), f32)], axis=0)
    left_s[...] = left.T.astype(bf16)
    right_s[...] = pair_right(pos).astype(bf16)
    pos_s[...] = pos

    least, most = [], []
    for s in range(slabs):
        at = slice(s * capacity, (s + 1) * capacity)
        least.append(jnp.min(jnp.where(used[:, at], x[:, at], FAR), axis=1, keepdims=True))
        most.append(jnp.max(jnp.where(used[:, at], x[:, at], -FAR), axis=1, keepdims=True))
    gap = jnp.full((1, 1), FAR, f32)
    for s in range(slabs - BAND):
        gap = jnp.minimum(gap, least[s + BAND] - most[s])
    close = gap[0, 0] < 1.0

    def run(band):
        span = min(slabs, 2 * band + 2)
        rows = slice(0, span * capacity)

        def place(tile):
            start = jnp.clip(2 * tile - band, 0, slabs - span)
            at = pl.ds(pl.multiple_of(start * capacity, capacity), span * capacity)
            return at, pl.ds(pl.multiple_of(tile * pair, pair), pair)

        def fill(tile, carry):
            at, lanes = place(tile)
            near = jnp.dot(left_s[at, 0:48], right_s[:, lanes], preferred_element_type=f32)
            near = jnp.maximum(near, 0.0)
            weight = near * near
            rho_s[:, lanes] = jnp.sum(weight, axis=0, keepdims=True)
            square = weight * weight
            high = square.astype(bf16)
            high_s[tile, rows] = high
            low_s[tile, rows] = (square - high.astype(f32)).astype(bf16)
            return carry

        lax.fori_loop(0, slabs // 2, fill, 0, unroll=2)
        pos = pos_s[...]
        row = lax.broadcasted_iota(jnp.int32, pos.shape, 0)
        base = jnp.where(row == 3, 0.0, pos)
        blocks = [*thirds(base), *thirds(base * rho_s[...])]
        terms_s[...] = jnp.concatenate([blocks[i] for i in (0, 3, 1, 4, 2, 5)], axis=0).astype(bf16)

        def push(tile, carry):
            at, lanes = place(tile)
            total = jnp.dot(terms_s[:, at], high_s[tile, rows], preferred_element_type=f32)
            small = jnp.dot(terms_s[0:16, at], low_s[tile, rows], preferred_element_type=f32)
            total = total[0:16] + (total[16:32] + (total[32:48] + small))
            here = pos_s[0:3, lanes]
            plain = here * total[4:5] - total[0:3]
            dense = here * total[12:13] - total[8:11]
            force = f32(2.0 * BODY_SCALE) * (rho_s[:, lanes] * plain + dense)
            out_ref[2 * tile, 0:3, :] = force[:, :capacity]
            out_ref[2 * tile + 1, 0:3, :] = force[:, capacity:]
            return carry

        lax.fori_loop(0, slabs // 2, push, 0, unroll=2)

    pl.when(close)(lambda: run(BAND))
    pl.when(jnp.logical_not(close))(lambda: run(BAND - 1))
    out_ref[:, 3, :] = jnp.zeros((slabs, capacity), f32)


def body_forces(inbox, after):
    slabs, _, capacity = inbox.shape
    total = slabs * capacity
    span = min(slabs, 2 * BAND + 2)
    return pl.pallas_call(
        functools.partial(body_kernel, slabs),
        out_shape=jax.ShapeDtypeStruct((slabs, 4, capacity), f32),
        in_specs=[pl.BlockSpec(memory_space=VMEM), pl.BlockSpec(memory_space=pl.ANY)],
        out_specs=pl.BlockSpec(memory_space=VMEM),
        scratch_shapes=[
            VMEM((8, total), f32),
            VMEM((total, 64), bf16),
            VMEM((48, total), bf16),
            VMEM((48, total), bf16),
            VMEM((slabs // 2, span * capacity, 2 * capacity), bf16),
            VMEM((slabs // 2, span * capacity, 2 * capacity), bf16),
            VMEM((1, total), f32),
        ],
        compiler_params=pltpu.CompilerParams(vmem_limit_bytes=40 << 20),
        cost_estimate=pl.CostEstimate(flops=1 << 32, bytes_accessed=1 << 18, transcendentals=0),
    )(inbox, after)


def share_table(ring, beads_dev):
    table = contract_table()
    shares = np.zeros((ring, beads_dev, 2 * ring), np.float32)
    for p in range(ring):
        mine = slice(p * beads_dev, (p + 1) * beads_dev)
        for d in range(ring):
            shares[p, :, d] = table[(p + d) % ring, mine]
            shares[p, :, ring + d] = table[(p - d) % ring, mine] * np.float32(BEADS / CONTRACTED)
    return jnp.asarray(shares)


def first_kernel(ring, centroid_ref, offsets_ref, table_ref, q_ref, *part_refs):
    table = table_ref[lax.axis_index("bead")]
    for c in range(3):
        scaled = centroid_ref[c : c + 1, :] * f32(SLAB_SIDE if c else 1.0)
        q = scaled + offsets_ref[c]
        q_ref[c] = q
        for d in range(ring):
            part_refs[d][c : c + 1, :] = jnp.sum(table[:, d : d + 1] * q, axis=0, keepdims=True)


def first_step(centroid, offsets, table, ring):
    part = jax.ShapeDtypeStruct(centroid.shape, f32)
    return pl.pallas_call(
        functools.partial(first_kernel, ring),
        out_shape=(jax.ShapeDtypeStruct(offsets.shape, f32),) + (part,) * ring,
        in_specs=[pl.BlockSpec(memory_space=VMEM)] * 3,
        out_specs=(pl.BlockSpec(memory_space=VMEM),) * (1 + ring),
        compiler_params=pltpu.CompilerParams(vmem_limit_bytes=8 << 20),
        cost_estimate=pl.CostEstimate(flops=1 << 28, bytes_accessed=1 << 19, transcendentals=0),
    )(centroid, offsets, table)


def last_kernel(ring, force_ref, react_ref, table_ref, *refs):
    table = table_ref[lax.axis_index("bead")]
    *many_refs, out_ref = refs
    for c in range(3):
        total = force_ref[c] + react_ref[c]
        for d in range(ring):
            total = total + table[:, ring + d : ring + d + 1] * many_refs[d][c : c + 1, :]
        out_ref[c] = total


def last_step(force, react, table, many):
    return pl.pallas_call(
        functools.partial(last_kernel, len(many)),
        out_shape=jax.ShapeDtypeStruct(force.shape, f32),
        in_specs=[pl.BlockSpec(memory_space=VMEM)] * (3 + len(many)),
        out_specs=pl.BlockSpec(memory_space=VMEM),
        compiler_params=pltpu.CompilerParams(vmem_limit_bytes=8 << 20),
        cost_estimate=pl.CostEstimate(flops=1 << 28, bytes_accessed=1 << 19, transcendentals=0),
    )(force, react, table, *many)


def shards(centroid, bead_offsets, routes):
    beads_dev, _, mols = bead_offsets.shape
    domains = lax.axis_size("space")
    ring = lax.axis_size("bead")
    capacity = 2 * mols // domains
    half = beads_dev // 2
    table = share_table(ring, beads_dev)
    q, *parts = first_step(centroid, bead_offsets.transpose(1, 0, 2), table, ring)
    nxt = passed_along(q, "space", -1)
    parts = parts[:1] + [passed_along(parts[by], "bead", by) for by in range(1, ring)]

    force = self_pairs(q, None, 0, half)
    route = routes.reshape(1, mols)
    outbox, slot = routed(parts, route, domains, capacity, force)
    inbox = lax.all_to_all(outbox, "space", split_axis=0, concat_axis=0, tiled=True)
    force, react = cross_pairs(q, nxt, force, jnp.zeros_like(q), 0, half, (outbox,))
    bodies = body_forces(inbox, force)
    returned = lax.all_to_all(bodies, "space", split_axis=0, concat_axis=0, tiled=True)
    force, react = cross_pairs(q, nxt, force, react, half, half, (bodies,))
    mine = unrouted(returned, route, slot, force)
    arrived = passed_along(react, "space", 1)
    every = [mine] + [passed_along(mine, "bead", by) for by in range(1, ring)]
    force = self_pairs(q, force, half, half, (mine,))
    return last_step(force, arrived, table, every).transpose(1, 0, 2)


def solution(mesh):
    placed = (P(None, "space"), P("bead", None, "space"), P("space", None))
    return jax.shard_map(
        shards, mesh=mesh, in_specs=placed, out_specs=P("bead", None, "space"), check_vma=False
    )
```

```python
import functools
import math

import jax
import jax.numpy as jnp
from jax import lax
from jax.experimental import pallas as pl
from jax.experimental.pallas import tpu as pltpu
from jax.sharding import PartitionSpec as P

BEADS = 32
CONTRACTED = 4
PAIR_SCALE = 0.1
BODY_SCALE = 0.1
SLAB_SIDE = 1.5
BAND = 4
FAR = 64.0


f32, bf16 = jnp.float32, jnp.bfloat16
VMEM = pltpu.VMEM


def passed_along(value, axis, by):
    peers = lax.axis_size(axis)
    return lax.ppermute(value, axis, [(i, (i + by) % peers) for i in range(peers)])


def thirds(x):
    high = x.astype(bf16).astype(f32)
    rest = x - high
    mid = rest.astype(bf16).astype(f32)
    return high, mid, rest - mid


CROSS_ROWS = 512
SELF_ROWS = 256
LANES = 128


def with_norm(q):
    mols = q.shape[-1]
    norm = 0.5 - jnp.sum(q * q, axis=0, keepdims=True)
    return jnp.concatenate([q, norm, jnp.ones((1, mols), f32), jnp.zeros((3, mols), f32)], axis=0)


def centred(ref, bead, shift):
    mids = (0.5 - shift, 0.5 * SLAB_SIDE, 0.5 * SLAB_SIDE)
    return with_norm(jnp.concatenate([ref[c, pl.ds(bead, 1), :] - f32(mids[c]) for c in range(3)], axis=0))


def pair_left(p, fine=False):
    row = lax.broadcasted_iota(jnp.int32, p.shape, 0)
    high, mid, low = thirds(p)
    place, norm, one = row < 3, row == 3, row == 4
    blocks = [
        high,
        jnp.where(norm, mid, high),
        jnp.where(norm, low, jnp.where(one, 1.0, mid)),
        jnp.where(place, mid, 0.0),
    ]
    if fine:
        blocks += [jnp.where(place, high, 0.0), jnp.where(place, low, 0.0)]
    return jnp.concatenate(blocks, axis=0)


def pair_right(p, fine=False):
    row = lax.broadcasted_iota(jnp.int32, p.shape, 0)
    high, mid, low = thirds(p)
    place, norm, one = row < 3, row == 3, row == 4

    def both(x, part):
        rest = jnp.where(norm, 1.0, jnp.where(one, part[3:4], 0.0))
        return jnp.where(place, 2.0 * x, rest)

    blocks = [both(high, high), both(mid, mid), both(high, low), jnp.where(place, 2.0 * mid, 0.0)]
    if fine:
        blocks += [jnp.where(place, 2.0 * low, 0.0), jnp.where(place, 2.0 * high, 0.0)]
    return jnp.concatenate(blocks, axis=0)


def pair_terms(p):
    row = lax.broadcasted_iota(jnp.int32, p.shape, 0)
    high, mid, _ = thirds(p)
    return jnp.concatenate([high, jnp.where(row < 3, mid, 0.0)], axis=0).astype(bf16)


def put_left(left_s, p):
    left_s[...] = pair_left(p).T.astype(bf16)


def weigh(left_s, right_s, weight_s, slot, block, lane, count):
    rows = weight_s.shape[2]
    at = pl.ds(pl.multiple_of(block * rows, rows), rows)
    lanes = slice(lane * LANES, (lane + count) * LANES)
    soft = jnp.dot(left_s[at, :], right_s[:, lanes], preferred_element_type=f32)
    soft = jnp.maximum(soft, 0.0)
    weight = (soft * soft).astype(bf16)
    for k in range(count):
        weight_s[slot, lane + k] = weight[:, k * LANES : (k + 1) * LANES]


def turn(weight_s, turned_s, slot, lane):
    turned = weight_s[slot, lane].T
    for k in range(turned.shape[1] // LANES):
        turned_s[slot, k, lane * LANES : (lane + 1) * LANES, :] = turned[:, k * LANES : (k + 1) * LANES]


def wide(ref, slot, lane, rows=slice(None)):
    return jnp.concatenate([ref[slot, lane, rows, :], ref[slot, lane + 1, rows, :]], axis=1)


def force_of(p, acc):
    return (p[0:3] * acc[4:5] - (acc[0:3] + acc[8:11])) * f32(6.0 * PAIR_SCALE)


def add_rows(out_ref, bead, force):
    for c in range(3):
        out_ref[c, pl.ds(bead, 1), :] += force[c : c + 1]


def cross_kernel(first, n_after, own_ref, next_ref, *refs):
    base_ref, react_in_ref = refs[0:2]
    out_ref, react_ref = refs[2 + n_after : 4 + n_after]
    left_s, right_s, own_s, next_s, weight_s, turned_s, acc_s, react_s = refs[4 + n_after :]
    mols = own_ref.shape[-1]

    @pl.when(pl.program_id(0) == 0)
    def _():
        out_ref[...] = base_ref[...]
        react_ref[...] = react_in_ref[...]

    bead = pl.program_id(0) + first
    own, nxt = centred(own_ref, bead, 0.0), centred(next_ref, bead, 1.0)
    right_s[...] = pair_right(own).astype(bf16)
    put_left(left_s, nxt)
    own_s[...], next_s[...] = pair_terms(own), pair_terms(nxt)
    tiles, steps = mols // LANES, mols // CROSS_ROWS
    group = min(8, tiles)

    def fill(step, slot):
        for lane in range(0, tiles, group):
            weigh(left_s, right_s, weight_s, slot, step, lane, group)

    def push(step, slot, fresh=False):
        terms = next_s[:, pl.ds(pl.multiple_of(step * CROSS_ROWS, CROSS_ROWS), CROSS_ROWS)]
        for lane in range(0, tiles, 2):
            part = jnp.dot(terms, wide(weight_s, slot, lane), preferred_element_type=f32)
            lanes = slice(lane * LANES, (lane + 2) * LANES)
            if fresh:
                acc_s[:, lanes] = part
            else:
                acc_s[:, lanes] += part

    def flip(slot):
        for lane in range(tiles):
            turn(weight_s, turned_s, slot, lane)

    def back(step, slot):
        at = pl.ds(pl.multiple_of(step * CROSS_ROWS, CROSS_ROWS), CROSS_ROWS)
        turned = jnp.concatenate([turned_s[slot, k] for k in range(CROSS_ROWS // LANES)], axis=1)
        react_s[:, at] = jnp.dot(own_s[...], turned, preferred_element_type=f32)

    fill(0, 0)
    fill(1, 1)
    push(0, 0, True)
    flip(0)

    def two_steps(turn_no, carry):
        step = 2 * turn_no + 1
        fill(step + 1, 0)
        push(step, 1)
        flip(1)
        back(step - 1, 0)
        fill(step + 2, 1)
        push(step + 1, 0)
        flip(0)
        back(step, 1)
        return carry

    lax.fori_loop(0, (steps - 2) // 2, two_steps, 0)
    push(steps - 1, 1)
    flip(1)
    back(steps - 2, 0)
    back(steps - 1, 1)
    add_rows(out_ref, bead, force_of(own, acc_s[...]))
    add_rows(react_ref, bead, force_of(nxt, react_s[...]))


def self_kernel(first, n_after, fresh, own_ref, *refs):
    base_ref = None if fresh else refs[0]
    skip = n_after + (0 if fresh else 1)
    out_ref, left_s, right_s, own_s, weight_s, turned_s, acc_s = refs[skip:]
    mols = own_ref.shape[-1]

    @pl.when(pl.program_id(0) == 0)
    def _():
        out_ref[...] = jnp.zeros_like(out_ref) if fresh else base_ref[...]

    bead = pl.program_id(0) + first
    own = centred(own_ref, bead, 0.0)
    right_s[...] = pair_right(own).astype(bf16)
    put_left(left_s, own)
    own_s[...] = pair_terms(own)
    acc_s[...] = jnp.zeros_like(acc_s)
    tiles, steps = mols // LANES, mols // SELF_ROWS

    for step in range(steps + 2):
        if step < steps:
            for lane in range(2 * step, tiles, 2):
                weigh(left_s, right_s, weight_s, step % 2, step, lane, 2)
        now = step - 1
        if 0 <= now < steps:
            terms = own_s[:, now * SELF_ROWS : (now + 1) * SELF_ROWS]
            for lane in range(2 * now, tiles, 2):
                lanes = slice(lane * LANES, (lane + 2) * LANES)
                acc_s[:, lanes] += jnp.dot(terms, wide(weight_s, now % 2, lane), preferred_element_type=f32)
            for lane in range(2 * now + 2, tiles):
                turn(weight_s, turned_s, now % 2, lane)
        now = step - 2
        if 0 <= now < steps - 1:
            rows = slice((now + 1) * SELF_ROWS, mols)
            part = jnp.dot(own_s[:, rows], wide(turned_s, now % 2, 0, rows), preferred_element_type=f32)
            acc_s[:, now * SELF_ROWS : (now + 1) * SELF_ROWS] += part
    add_rows(out_ref, bead, force_of(own, acc_s[...]))


def pair_call(kernel, arrays, after, outs, count, n_terms, n_acc, side):
    mols = arrays[0].shape[-1]
    flops = count * mols * mols * 3200 * outs // 2
    whole = pl.BlockSpec(arrays[0].shape, lambda b: (0, 0, 0))
    shape = jax.ShapeDtypeStruct(arrays[0].shape, f32)
    return pl.pallas_call(
        kernel,
        grid=(count,),
        out_shape=(shape,) * outs,
        in_specs=[whole] * len(arrays) + [pl.BlockSpec(memory_space=pl.ANY)] * len(after),
        out_specs=(whole,) * outs,
        scratch_shapes=[
            VMEM((mols, 32), bf16),
            VMEM((32, mols), bf16),
            *[VMEM((16, mols), bf16)] * n_terms,
            VMEM((2, mols // LANES, side, LANES), bf16),
            VMEM((2, side // LANES, mols, LANES), bf16),
            *[VMEM((16, mols), f32)] * n_acc,
        ],
        compiler_params=pltpu.CompilerParams(vmem_limit_bytes=24 << 20),
        cost_estimate=pl.CostEstimate(flops=flops, bytes_accessed=1 << 20, transcendentals=0),
    )(*arrays, *after)


def cross_pairs(own, nxt, base, react, first, count, after=()):
    kernel = functools.partial(cross_kernel, first, len(after))
    return pair_call(kernel, [own, nxt, base, react], after, 2, count, 2, 2, CROSS_ROWS)


def self_pairs(own, base, first, count, after=()):
    kernel = functools.partial(self_kernel, first, len(after), base is None)
    arrays = [own] if base is None else [own, base]
    return pair_call(kernel, arrays, after, 1, count, 1, 1, SELF_ROWS)[0]


def named(route, domains):
    return (lax.broadcasted_iota(jnp.int32, (domains, route.shape[1]), 0) == route).astype(f32)


def chosen(slot, capacity):
    return (lax.broadcasted_iota(jnp.int32, (capacity, slot.shape[1]), 0) == slot).astype(bf16)


def route_kernel(capacity, *refs):
    *part_refs, route_ref, _, out_ref, slot_ref, rows_s = refs
    pos = sum(ref[...] for ref in part_refs)
    mols = pos.shape[-1]
    domains = out_ref.shape[0]
    mine = named(route_ref[...], domains)
    width = 128
    up_to = (
        lax.broadcasted_iota(jnp.int32, (width, width), 0) <= lax.broadcasted_iota(jnp.int32, (width, width), 1)
    ).astype(bf16)
    before = jnp.zeros((domains, 1), f32)
    slots = []
    for lo in range(0, mols, width):
        piece = mine[:, lo : lo + width]
        rank = jnp.dot(piece.astype(bf16), up_to, preferred_element_type=f32)
        slots.append(jnp.sum(piece * (rank + before - 1.0), axis=0, keepdims=True))
        before = before + jnp.sum(piece, axis=1, keepdims=True)
    slot = jnp.concatenate(slots, axis=1).astype(jnp.int32)
    slot_ref[...] = slot
    at_slot = chosen(slot, capacity)
    for part, value in enumerate(thirds(pos)):
        for c in range(3):
            row = 3 * part + c
            rows_s[row * domains : (row + 1) * domains, :] = (mine * value[c : c + 1]).astype(bf16)
    rows_s[9 * domains :, :] = mine.astype(bf16)
    sent = lax.dot_general(rows_s[...], at_slot, (((1,), (1,)), ((), ())), preferred_element_type=f32)
    sent = sent.reshape(10, domains, capacity)
    for c in range(3):
        value = sent[c] + sent[3 + c] + sent[6 + c]
        if c == 1:
            value = value + FAR * (1.0 - sent[9])
        out_ref[:, c, :] = value
    out_ref[:, 3, :] = sent[9]


def routed(parts, route, domains, capacity, after):
    mols = route.shape[-1]
    return pl.pallas_call(
        functools.partial(route_kernel, capacity),
        out_shape=(jax.ShapeDtypeStruct((domains, 4, capacity), f32), jax.ShapeDtypeStruct((1, mols), jnp.int32)),
        in_specs=[pl.BlockSpec(memory_space=VMEM)] * (len(parts) + 1) + [pl.BlockSpec(memory_space=pl.ANY)],
        out_specs=(pl.BlockSpec(memory_space=VMEM),) * 2,
        scratch_shapes=[VMEM((10 * domains, mols), bf16)],
        compiler_params=pltpu.CompilerParams(vmem_limit_bytes=24 << 20),
        cost_estimate=pl.CostEstimate(flops=1 << 30, bytes_accessed=1 << 18, transcendentals=0),
    )(*parts, route, after)


def unroute_kernel(capacity, back_ref, route_ref, slot_ref, _, out_ref):
    domains = back_ref.shape[0]
    mine = named(route_ref[...], domains)
    at_slot = chosen(slot_ref[...], capacity)
    for c in range(3):
        rows = jnp.concatenate(thirds(back_ref[:, c, :]), axis=0).astype(bf16)
        spread = jnp.dot(rows, at_slot, preferred_element_type=f32)
        value = spread[:domains] + spread[domains : 2 * domains] + spread[2 * domains :]
        out_ref[c : c + 1, :] = jnp.sum(value * mine, axis=0, keepdims=True)


def unrouted(back, route, slot, after):
    mols = route.shape[-1]
    return pl.pallas_call(
        functools.partial(unroute_kernel, back.shape[-1]),
        out_shape=jax.ShapeDtypeStruct((3, mols), f32),
        in_specs=[pl.BlockSpec(memory_space=VMEM)] * 3 + [pl.BlockSpec(memory_space=pl.ANY)],
        out_specs=pl.BlockSpec(memory_space=VMEM),
        compiler_params=pltpu.CompilerParams(vmem_limit_bytes=24 << 20),
        cost_estimate=pl.CostEstimate(flops=1 << 29, bytes_accessed=1 << 18, transcendentals=0),
    )(back, route, slot, after)


def body_kernel(slabs, in_ref, _, out_ref, pos_s, left_s, right_s, terms_s, high_s, low_s, rho_s):
    capacity = in_ref.shape[-1]
    pair = 2 * capacity
    for s in range(slabs):
        pos_s[0:4, s * capacity : (s + 1) * capacity] = in_ref[s]
    lane = lax.broadcasted_iota(jnp.int32, (1, slabs * capacity), 1)
    slab = (lane // capacity).astype(f32) - 0.5 * slabs
    x = 0.5 * (pos_s[0:1, :] + slab)
    yz = 0.5 * (pos_s[1:3, :] - 0.5 * SLAB_SIDE)
    used = pos_s[3:4, :] > 0.5
    pos = with_norm(jnp.concatenate([x, yz], axis=0))
    left = jnp.concatenate([pair_left(pos, True), jnp.zeros((16, pos.shape[1]), f32)], axis=0)
    left_s[...] = left.T.astype(bf16)
    right_s[...] = pair_right(pos, True).astype(bf16)
    pos_s[...] = pos

    least, most = [], []
    for s in range(slabs):
        at = slice(s * capacity, (s + 1) * capacity)
        least.append(jnp.min(jnp.where(used[:, at], x[:, at], FAR), axis=1, keepdims=True))
        most.append(jnp.max(jnp.where(used[:, at], x[:, at], -FAR), axis=1, keepdims=True))
    gap = jnp.full((1, 1), FAR, f32)
    for s in range(slabs - BAND):
        gap = jnp.minimum(gap, least[s + BAND] - most[s])
    close = gap[0, 0] < 1.0

    def run(band):
        span = min(slabs, 2 * band + 2)
        rows = slice(0, span * capacity)

        def place(tile):
            start = jnp.clip(2 * tile - band, 0, slabs - span)
            at = pl.ds(pl.multiple_of(start * capacity, capacity), span * capacity)
            return at, pl.ds(pl.multiple_of(tile * pair, pair), pair)

        def fill(tile, carry):
            at, lanes = place(tile)
            near = jnp.dot(left_s[at, 0:48], right_s[:, lanes], preferred_element_type=f32)
            near = jnp.maximum(near, 0.0)
            weight = near * near
            rho_s[:, lanes] = jnp.sum(weight, axis=0, keepdims=True)
            square = weight * weight
            high = square.astype(bf16)
            high_s[tile, rows] = high
            low_s[tile, rows] = (square - high.astype(f32)).astype(bf16)
            return carry

        lax.fori_loop(0, slabs // 2, fill, 0, unroll=2)
        pos = pos_s[...]
        row = lax.broadcasted_iota(jnp.int32, pos.shape, 0)
        base = jnp.where(row == 3, 0.0, pos)
        blocks = [*thirds(base), *thirds(base * rho_s[...])]
        terms_s[...] = jnp.concatenate([blocks[i] for i in (0, 3, 1, 4, 2, 5)], axis=0).astype(bf16)

        def push(tile, carry):
            at, lanes = place(tile)
            total = jnp.dot(terms_s[:, at], high_s[tile, rows], preferred_element_type=f32)
            small = jnp.dot(terms_s[0:16, at], low_s[tile, rows], preferred_element_type=f32)
            total = total[0:16] + (total[16:32] + (total[32:48] + small))
            here = pos_s[0:3, lanes]
            plain = here * total[4:5] - total[0:3]
            dense = here * total[12:13] - total[8:11]
            force = f32(2.0 * BODY_SCALE) * (rho_s[:, lanes] * plain + dense)
            out_ref[2 * tile, 0:3, :] = force[:, :capacity]
            out_ref[2 * tile + 1, 0:3, :] = force[:, capacity:]
            return carry

        lax.fori_loop(0, slabs // 2, push, 0, unroll=2)

    pl.when(close)(lambda: run(BAND))
    pl.when(jnp.logical_not(close))(lambda: run(BAND - 1))
    out_ref[:, 3, :] = jnp.zeros((slabs, capacity), f32)


def body_forces(inbox, after):
    slabs, _, capacity = inbox.shape
    total = slabs * capacity
    span = min(slabs, 2 * BAND + 2)
    return pl.pallas_call(
        functools.partial(body_kernel, slabs),
        out_shape=jax.ShapeDtypeStruct((slabs, 4, capacity), f32),
        in_specs=[pl.BlockSpec(memory_space=VMEM), pl.BlockSpec(memory_space=pl.ANY)],
        out_specs=pl.BlockSpec(memory_space=VMEM),
        scratch_shapes=[
            VMEM((8, total), f32),
            VMEM((total, 64), bf16),
            VMEM((48, total), bf16),
            VMEM((48, total), bf16),
            VMEM((slabs // 2, span * capacity, 2 * capacity), bf16),
            VMEM((slabs // 2, span * capacity, 2 * capacity), bf16),
            VMEM((1, total), f32),
        ],
        compiler_params=pltpu.CompilerParams(vmem_limit_bytes=40 << 20),
        cost_estimate=pl.CostEstimate(flops=1 << 32, bytes_accessed=1 << 18, transcendentals=0),
    )(inbox, after)


def shares(ring, beads_dev, sign):
    place = lax.axis_index("bead")
    bead = place * beads_dev + lax.broadcasted_iota(jnp.int32, (beads_dev, ring), 0)
    coarse = lax.rem(place + ring + sign * lax.broadcasted_iota(jnp.int32, (beads_dev, ring), 1), ring)
    phase = 2.0 * math.pi * (bead.astype(f32) / BEADS - coarse.astype(f32) / CONTRACTED)
    return (1.0 + 2.0 * jnp.cos(phase)) / BEADS


def first_kernel(ring, centroid_ref, offsets_ref, q_ref, *part_refs):
    table = shares(ring, offsets_ref.shape[1], 1)
    for c in range(3):
        scaled = centroid_ref[c : c + 1, :] * f32(SLAB_SIDE if c else 1.0)
        q = scaled + offsets_ref[c]
        q_ref[c] = q
        for d in range(ring):
            part_refs[d][c : c + 1, :] = jnp.sum(table[:, d : d + 1] * q, axis=0, keepdims=True)


def first_step(centroid, offsets, ring):
    part = jax.ShapeDtypeStruct(centroid.shape, f32)
    return pl.pallas_call(
        functools.partial(first_kernel, ring),
        out_shape=(jax.ShapeDtypeStruct(offsets.shape, f32),) + (part,) * ring,
        in_specs=[pl.BlockSpec(memory_space=VMEM)] * 2,
        out_specs=(pl.BlockSpec(memory_space=VMEM),) * (1 + ring),
        compiler_params=pltpu.CompilerParams(vmem_limit_bytes=8 << 20),
        cost_estimate=pl.CostEstimate(flops=1 << 28, bytes_accessed=1 << 19, transcendentals=0),
    )(centroid, offsets)


def last_kernel(ring, force_ref, react_ref, *refs):
    table = shares(ring, force_ref.shape[1], -1) * f32(BEADS / CONTRACTED)
    *many_refs, out_ref = refs
    for c in range(3):
        total = force_ref[c] + react_ref[c]
        for d in range(ring):
            total = total + table[:, d : d + 1] * many_refs[d][c : c + 1, :]
        out_ref[c] = total


def last_step(force, react, many):
    return pl.pallas_call(
        functools.partial(last_kernel, len(many)),
        out_shape=jax.ShapeDtypeStruct(force.shape, f32),
        in_specs=[pl.BlockSpec(memory_space=VMEM)] * (2 + len(many)),
        out_specs=pl.BlockSpec(memory_space=VMEM),
        compiler_params=pltpu.CompilerParams(vmem_limit_bytes=8 << 20),
        cost_estimate=pl.CostEstimate(flops=1 << 28, bytes_accessed=1 << 19, transcendentals=0),
    )(force, react, *many)


def shards(centroid, bead_offsets, routes):
    beads_dev, _, mols = bead_offsets.shape
    domains = lax.axis_size("space")
    ring = lax.axis_size("bead")
    capacity = 2 * mols // domains
    half = beads_dev // 2
    q, *parts = first_step(centroid, bead_offsets.transpose(1, 0, 2), ring)
    nxt = passed_along(q, "space", -1)
    parts = parts[:1] + [passed_along(parts[by], "bead", by) for by in range(1, ring)]

    force = self_pairs(q, None, 0, half)
    route = routes.reshape(1, mols)
    outbox, slot = routed(parts, route, domains, capacity, force)
    inbox = lax.all_to_all(outbox, "space", split_axis=0, concat_axis=0, tiled=True)
    force, react = cross_pairs(q, nxt, force, jnp.zeros_like(q), 0, half, (outbox,))
    bodies = body_forces(inbox, force)
    returned = lax.all_to_all(bodies, "space", split_axis=0, concat_axis=0, tiled=True)
    force, react = cross_pairs(q, nxt, force, react, half, half, (bodies,))
    mine = unrouted(returned, route, slot, force)
    arrived = passed_along(react, "space", 1)
    every = [mine] + [passed_along(mine, "bead", by) for by in range(1, ring)]
    force = self_pairs(q, force, half, half, (mine,))
    return last_step(force, arrived, every).transpose(1, 0, 2)


def solution(mesh):
    placed = (P(None, "space"), P("bead", None, "space"), P("space", None))
    return jax.shard_map(
        shards, mesh=mesh, in_specs=placed, out_specs=P("bead", None, "space"), check_vma=False
    )
```

```python
import functools
import math

import jax
import jax.numpy as jnp
from jax import lax
from jax.experimental import pallas as pl
from jax.experimental.pallas import tpu as pltpu
from jax.sharding import PartitionSpec as P

BEADS = 32
CONTRACTED = 4
PAIR_SCALE = 0.1
BODY_SCALE = 0.1
SLAB_SIDE = 1.5
BAND = 4
FAR = 64.0


f32, bf16 = jnp.float32, jnp.bfloat16
VMEM = pltpu.VMEM


def passed_along(value, axis, by):
    peers = lax.axis_size(axis)
    return lax.ppermute(value, axis, [(i, (i + by) % peers) for i in range(peers)])


def thirds(x):
    high = x.astype(bf16).astype(f32)
    rest = x - high
    mid = rest.astype(bf16).astype(f32)
    return high, mid, rest - mid


CROSS_ROWS = 512
SELF_ROWS = 256
LANES = 128


def with_norm(q):
    mols = q.shape[-1]
    norm = 0.5 - jnp.sum(q * q, axis=0, keepdims=True)
    return jnp.concatenate([q, norm, jnp.ones((1, mols), f32), jnp.zeros((3, mols), f32)], axis=0)


def centred(ref, bead, shift):
    mids = (0.5 - shift, 0.5 * SLAB_SIDE, 0.5 * SLAB_SIDE)
    return with_norm(jnp.concatenate([ref[c, pl.ds(bead, 1), :] - f32(mids[c]) for c in range(3)], axis=0))


def pair_left(p, fine=False):
    row = lax.broadcasted_iota(jnp.int32, p.shape, 0)
    high, mid, low = thirds(p)
    place, norm, one = row < 3, row == 3, row == 4
    blocks = [
        high,
        jnp.where(norm, mid, high),
        jnp.where(norm, low, jnp.where(one, 1.0, mid)),
        jnp.where(place, mid, 0.0),
    ]
    if fine:
        blocks += [jnp.where(place, high, 0.0), jnp.where(place, low, 0.0)]
    return jnp.concatenate(blocks, axis=0)


def pair_right(p, fine=False):
    row = lax.broadcasted_iota(jnp.int32, p.shape, 0)
    high, mid, low = thirds(p)
    place, norm, one = row < 3, row == 3, row == 4

    def both(x, part):
        rest = jnp.where(norm, 1.0, jnp.where(one, part[3:4], 0.0))
        return jnp.where(place, 2.0 * x, rest)

    blocks = [both(high, high), both(mid, mid), both(high, low), jnp.where(place, 2.0 * mid, 0.0)]
    if fine:
        blocks += [jnp.where(place, 2.0 * low, 0.0), jnp.where(place, 2.0 * high, 0.0)]
    return jnp.concatenate(blocks, axis=0)


def pair_terms(p):
    row = lax.broadcasted_iota(jnp.int32, p.shape, 0)
    high, mid, _ = thirds(p)
    return jnp.concatenate([high, jnp.where(row < 3, mid, 0.0)], axis=0).astype(bf16)


def put_left(left_s, p):
    left_s[...] = pair_left(p).T.astype(bf16)


def weigh(left_s, right_s, weight_s, slot, block, lane, count):
    rows = weight_s.shape[2]
    at = pl.ds(pl.multiple_of(block * rows, rows), rows)
    lanes = slice(lane * LANES, (lane + count) * LANES)
    soft = jnp.dot(left_s[at, :], right_s[:, lanes], preferred_element_type=f32)
    soft = jnp.maximum(soft, 0.0)
    weight = (soft * soft).astype(bf16)
    for k in range(count):
        weight_s[slot, lane + k] = weight[:, k * LANES : (k + 1) * LANES]


def turn(weight_s, turned_s, slot, lane):
    turned = weight_s[slot, lane].T
    for k in range(turned.shape[1] // LANES):
        turned_s[slot, k, lane * LANES : (lane + 1) * LANES, :] = turned[:, k * LANES : (k + 1) * LANES]


def wide(ref, slot, lane, rows=slice(None)):
    return jnp.concatenate([ref[slot, lane, rows, :], ref[slot, lane + 1, rows, :]], axis=1)


def force_of(p, acc):
    return (p[0:3] * acc[4:5] - (acc[0:3] + acc[8:11])) * f32(6.0 * PAIR_SCALE)


def add_rows(out_ref, bead, force):
    for c in range(3):
        out_ref[c, pl.ds(bead, 1), :] += force[c : c + 1]


def cross_kernel(first, n_after, own_ref, next_ref, *refs):
    base_ref, react_in_ref = refs[0:2]
    out_ref, react_ref = refs[2 + n_after : 4 + n_after]
    left_s, right_s, own_s, next_s, weight_s, turned_s, acc_s, react_s = refs[4 + n_after :]
    mols = own_ref.shape[-1]

    @pl.when(pl.program_id(0) == 0)
    def _():
        out_ref[...] = base_ref[...]
        react_ref[...] = react_in_ref[...]

    bead = pl.program_id(0) + first
    own, nxt = centred(own_ref, bead, 0.0), centred(next_ref, bead, 1.0)
    right_s[...] = pair_right(own).astype(bf16)
    put_left(left_s, nxt)
    own_s[...], next_s[...] = pair_terms(own), pair_terms(nxt)
    tiles, steps = mols // LANES, mols // CROSS_ROWS
    group = min(8, tiles)

    def fill(step, slot):
        for lane in range(0, tiles, group):
            weigh(left_s, right_s, weight_s, slot, step, lane, group)

    def push(step, slot, fresh=False):
        terms = next_s[:, pl.ds(pl.multiple_of(step * CROSS_ROWS, CROSS_ROWS), CROSS_ROWS)]
        for lane in range(0, tiles, 2):
            part = jnp.dot(terms, wide(weight_s, slot, lane), preferred_element_type=f32)
            lanes = slice(lane * LANES, (lane + 2) * LANES)
            if fresh:
                acc_s[:, lanes] = part
            else:
                acc_s[:, lanes] += part

    def flip(slot):
        for lane in range(tiles):
            turn(weight_s, turned_s, slot, lane)

    def back(step, slot):
        at = pl.ds(pl.multiple_of(step * CROSS_ROWS, CROSS_ROWS), CROSS_ROWS)
        turned = jnp.concatenate([turned_s[slot, k] for k in range(CROSS_ROWS // LANES)], axis=1)
        react_s[:, at] = jnp.dot(own_s[...], turned, preferred_element_type=f32)

    fill(0, 0)
    fill(1, 1)
    push(0, 0, True)
    flip(0)

    def two_steps(turn_no, carry):
        step = 2 * turn_no + 1
        fill(step + 1, 0)
        push(step, 1)
        flip(1)
        back(step - 1, 0)
        fill(step + 2, 1)
        push(step + 1, 0)
        flip(0)
        back(step, 1)
        return carry

    lax.fori_loop(0, (steps - 2) // 2, two_steps, 0)
    push(steps - 1, 1)
    flip(1)
    back(steps - 2, 0)
    back(steps - 1, 1)
    add_rows(out_ref, bead, force_of(own, acc_s[...]))
    add_rows(react_ref, bead, force_of(nxt, react_s[...]))


def self_kernel(first, n_after, fresh, own_ref, *refs):
    base_ref = None if fresh else refs[0]
    skip = n_after + (0 if fresh else 1)
    out_ref, left_s, right_s, own_s, weight_s, turned_s, acc_s = refs[skip:]
    mols = own_ref.shape[-1]

    @pl.when(pl.program_id(0) == 0)
    def _():
        out_ref[...] = jnp.zeros_like(out_ref) if fresh else base_ref[...]

    bead = pl.program_id(0) + first
    own = centred(own_ref, bead, 0.0)
    right_s[...] = pair_right(own).astype(bf16)
    put_left(left_s, own)
    own_s[...] = pair_terms(own)
    acc_s[...] = jnp.zeros_like(acc_s)
    tiles, steps = mols // LANES, mols // SELF_ROWS

    for step in range(steps + 2):
        if step < steps:
            for lane in range(2 * step, tiles, 2):
                weigh(left_s, right_s, weight_s, step % 2, step, lane, 2)
        now = step - 1
        if 0 <= now < steps:
            terms = own_s[:, now * SELF_ROWS : (now + 1) * SELF_ROWS]
            for lane in range(2 * now, tiles, 2):
                lanes = slice(lane * LANES, (lane + 2) * LANES)
                acc_s[:, lanes] += jnp.dot(terms, wide(weight_s, now % 2, lane), preferred_element_type=f32)
            for lane in range(2 * now + 2, tiles):
                turn(weight_s, turned_s, now % 2, lane)
        now = step - 2
        if 0 <= now < steps - 1:
            rows = slice((now + 1) * SELF_ROWS, mols)
            part = jnp.dot(own_s[:, rows], wide(turned_s, now % 2, 0, rows), preferred_element_type=f32)
            acc_s[:, now * SELF_ROWS : (now + 1) * SELF_ROWS] += part
    add_rows(out_ref, bead, force_of(own, acc_s[...]))


def pair_call(kernel, arrays, after, outs, count, n_terms, n_acc, side):
    mols = arrays[0].shape[-1]
    flops = count * mols * mols * 3200 * outs // 2
    whole = pl.BlockSpec(arrays[0].shape, lambda b: (0, 0, 0))
    shape = jax.ShapeDtypeStruct(arrays[0].shape, f32)
    return pl.pallas_call(
        kernel,
        grid=(count,),
        out_shape=(shape,) * outs,
        in_specs=[whole] * len(arrays) + [pl.BlockSpec(memory_space=pl.ANY)] * len(after),
        out_specs=(whole,) * outs,
        scratch_shapes=[
            VMEM((mols, 32), bf16),
            VMEM((32, mols), bf16),
            *[VMEM((16, mols), bf16)] * n_terms,
            VMEM((2, mols // LANES, side, LANES), bf16),
            VMEM((2, side // LANES, mols, LANES), bf16),
            *[VMEM((16, mols), f32)] * n_acc,
        ],
        compiler_params=pltpu.CompilerParams(vmem_limit_bytes=24 << 20),
        cost_estimate=pl.CostEstimate(flops=flops, bytes_accessed=1 << 20, transcendentals=0),
    )(*arrays, *after)


def cross_pairs(own, nxt, base, react, first, count, after=()):
    kernel = functools.partial(cross_kernel, first, len(after))
    return pair_call(kernel, [own, nxt, base, react], after, 2, count, 2, 2, CROSS_ROWS)


def self_pairs(own, base, first, count, after=()):
    kernel = functools.partial(self_kernel, first, len(after), base is None)
    arrays = [own] if base is None else [own, base]
    return pair_call(kernel, arrays, after, 1, count, 1, 1, SELF_ROWS)[0]


def named(route, domains):
    return (lax.broadcasted_iota(jnp.int32, (domains, route.shape[1]), 0) == route).astype(f32)


def chosen(slot, capacity):
    return (lax.broadcasted_iota(jnp.int32, (capacity, slot.shape[1]), 0) == slot).astype(bf16)


def route_kernel(capacity, *refs):
    *part_refs, route_ref, _, out_ref, slot_ref, rows_s = refs
    pos = sum(ref[...] for ref in part_refs)
    mols = pos.shape[-1]
    domains = out_ref.shape[0]
    mine = named(route_ref[...], domains)
    width = 128
    up_to = (
        lax.broadcasted_iota(jnp.int32, (width, width), 0) <= lax.broadcasted_iota(jnp.int32, (width, width), 1)
    ).astype(bf16)
    before = jnp.zeros((domains, 1), f32)
    slots = []
    for lo in range(0, mols, width):
        piece = mine[:, lo : lo + width]
        rank = jnp.dot(piece.astype(bf16), up_to, preferred_element_type=f32)
        slots.append(jnp.sum(piece * (rank + before - 1.0), axis=0, keepdims=True))
        before = before + jnp.sum(piece, axis=1, keepdims=True)
    slot = jnp.concatenate(slots, axis=1).astype(jnp.int32)
    slot_ref[...] = slot
    at_slot = chosen(slot, capacity)
    for part, value in enumerate(thirds(pos)):
        for c in range(3):
            row = 3 * part + c
            rows_s[row * domains : (row + 1) * domains, :] = (mine * value[c : c + 1]).astype(bf16)
    rows_s[9 * domains :, :] = mine.astype(bf16)
    sent = lax.dot_general(rows_s[...], at_slot, (((1,), (1,)), ((), ())), preferred_element_type=f32)
    sent = sent.reshape(10, domains, capacity)
    for c in range(3):
        value = sent[c] + sent[3 + c] + sent[6 + c]
        if c == 1:
            value = value + FAR * (1.0 - sent[9])
        out_ref[:, c, :] = value
    out_ref[:, 3, :] = sent[9]


def routed(parts, route, domains, capacity, after):
    mols = route.shape[-1]
    return pl.pallas_call(
        functools.partial(route_kernel, capacity),
        out_shape=(jax.ShapeDtypeStruct((domains, 4, capacity), f32), jax.ShapeDtypeStruct((1, mols), jnp.int32)),
        in_specs=[pl.BlockSpec(memory_space=VMEM)] * (len(parts) + 1) + [pl.BlockSpec(memory_space=pl.ANY)],
        out_specs=(pl.BlockSpec(memory_space=VMEM),) * 2,
        scratch_shapes=[VMEM((10 * domains, mols), bf16)],
        compiler_params=pltpu.CompilerParams(vmem_limit_bytes=24 << 20),
        cost_estimate=pl.CostEstimate(flops=1 << 30, bytes_accessed=1 << 18, transcendentals=0),
    )(*parts, route, after)


def unroute_kernel(capacity, back_ref, route_ref, slot_ref, _, out_ref):
    domains = back_ref.shape[0]
    mine = named(route_ref[...], domains)
    at_slot = chosen(slot_ref[...], capacity)
    for c in range(3):
        rows = jnp.concatenate(thirds(back_ref[:, c, :]), axis=0).astype(bf16)
        spread = jnp.dot(rows, at_slot, preferred_element_type=f32)
        value = spread[:domains] + spread[domains : 2 * domains] + spread[2 * domains :]
        out_ref[c : c + 1, :] = jnp.sum(value * mine, axis=0, keepdims=True)


def unrouted(back, route, slot, after):
    mols = route.shape[-1]
    return pl.pallas_call(
        functools.partial(unroute_kernel, back.shape[-1]),
        out_shape=jax.ShapeDtypeStruct((3, mols), f32),
        in_specs=[pl.BlockSpec(memory_space=VMEM)] * 3 + [pl.BlockSpec(memory_space=pl.ANY)],
        out_specs=pl.BlockSpec(memory_space=VMEM),
        compiler_params=pltpu.CompilerParams(vmem_limit_bytes=24 << 20),
        cost_estimate=pl.CostEstimate(flops=1 << 29, bytes_accessed=1 << 18, transcendentals=0),
    )(back, route, slot, after)


def body_kernel(slabs, in_ref, _, out_ref, pos_s, left_s, right_s, terms_s, high_s, low_s, rho_s):
    capacity = in_ref.shape[-1]
    pair = 2 * capacity
    for s in range(slabs):
        pos_s[0:4, s * capacity : (s + 1) * capacity] = in_ref[s]
    lane = lax.broadcasted_iota(jnp.int32, (1, slabs * capacity), 1)
    slab = (lane // capacity).astype(f32) - 0.5 * slabs
    x = 0.5 * (pos_s[0:1, :] + slab)
    yz = 0.5 * (pos_s[1:3, :] - 0.5 * SLAB_SIDE)
    used = pos_s[3:4, :] > 0.5
    pos = with_norm(jnp.concatenate([x, yz], axis=0))
    left = jnp.concatenate([pair_left(pos, True), jnp.zeros((16, pos.shape[1]), f32)], axis=0)
    left_s[...] = left.T.astype(bf16)
    right_s[...] = pair_right(pos, True).astype(bf16)
    pos_s[...] = pos

    least, most = [], []
    for s in range(slabs):
        at = slice(s * capacity, (s + 1) * capacity)
        least.append(jnp.min(jnp.where(used[:, at], x[:, at], FAR), axis=1, keepdims=True))
        most.append(jnp.max(jnp.where(used[:, at], x[:, at], -FAR), axis=1, keepdims=True))
    gap = jnp.full((1, 1), FAR, f32)
    for s in range(slabs - BAND):
        gap = jnp.minimum(gap, least[s + BAND] - most[s])
    close = gap[0, 0] < 1.0

    def run(band):
        span = min(slabs, 2 * band + 2)
        rows = slice(0, span * capacity)

        def place(tile):
            start = jnp.clip(2 * tile - band, 0, slabs - span)
            at = pl.ds(pl.multiple_of(start * capacity, capacity), span * capacity)
            return at, pl.ds(pl.multiple_of(tile * pair, pair), pair)

        def fill(tile, carry):
            at, lanes = place(tile)
            near = jnp.dot(left_s[at, 0:48], right_s[:, lanes], preferred_element_type=f32)
            near = jnp.maximum(near, 0.0)
            weight = near * near
            rho_s[:, lanes] = jnp.sum(weight, axis=0, keepdims=True)
            square = weight * weight
            high = square.astype(bf16)
            high_s[tile, rows] = high
            low_s[tile, rows] = (square - high.astype(f32)).astype(bf16)
            return carry

        unroll = slabs // 2 if band < BAND else 1
        lax.fori_loop(0, slabs // 2, fill, 0, unroll=unroll)
        pos = pos_s[...]
        row = lax.broadcasted_iota(jnp.int32, pos.shape, 0)
        base = jnp.where(row == 3, 0.0, pos)
        blocks = [*thirds(base), *thirds(base * rho_s[...])]
        terms_s[...] = jnp.concatenate([blocks[i] for i in (0, 3, 1, 4, 2, 5)], axis=0).astype(bf16)

        def push(tile, carry):
            at, lanes = place(tile)
            total = jnp.dot(terms_s[:, at], high_s[tile, rows], preferred_element_type=f32)
            small = jnp.dot(terms_s[0:16, at], low_s[tile, rows], preferred_element_type=f32)
            total = total[0:16] + (total[16:32] + (total[32:48] + small))
            here = pos_s[0:3, lanes]
            plain = here * total[4:5] - total[0:3]
            dense = here * total[12:13] - total[8:11]
            force = f32(2.0 * BODY_SCALE) * (rho_s[:, lanes] * plain + dense)
            out_ref[2 * tile, 0:3, :] = force[:, :capacity]
            out_ref[2 * tile + 1, 0:3, :] = force[:, capacity:]
            return carry

        lax.fori_loop(0, slabs // 2, push, 0, unroll=unroll)

    pl.when(close)(lambda: run(BAND))
    pl.when(jnp.logical_not(close))(lambda: run(BAND - 1))
    out_ref[:, 3, :] = jnp.zeros((slabs, capacity), f32)


def body_forces(inbox, after):
    slabs, _, capacity = inbox.shape
    total = slabs * capacity
    span = min(slabs, 2 * BAND + 2)
    return pl.pallas_call(
        functools.partial(body_kernel, slabs),
        out_shape=jax.ShapeDtypeStruct((slabs, 4, capacity), f32),
        in_specs=[pl.BlockSpec(memory_space=VMEM), pl.BlockSpec(memory_space=pl.ANY)],
        out_specs=pl.BlockSpec(memory_space=VMEM),
        scratch_shapes=[
            VMEM((8, total), f32),
            VMEM((total, 64), bf16),
            VMEM((48, total), bf16),
            VMEM((48, total), bf16),
            VMEM((slabs // 2, span * capacity, 2 * capacity), bf16),
            VMEM((slabs // 2, span * capacity, 2 * capacity), bf16),
            VMEM((1, total), f32),
        ],
        compiler_params=pltpu.CompilerParams(vmem_limit_bytes=40 << 20),
        cost_estimate=pl.CostEstimate(flops=1 << 32, bytes_accessed=1 << 18, transcendentals=0),
    )(inbox, after)


def shares(ring, beads_dev, sign):
    place = lax.axis_index("bead")
    bead = place * beads_dev + lax.broadcasted_iota(jnp.int32, (beads_dev, ring), 0)
    coarse = lax.rem(place + ring + sign * lax.broadcasted_iota(jnp.int32, (beads_dev, ring), 1), ring)
    phase = 2.0 * math.pi * (bead.astype(f32) / BEADS - coarse.astype(f32) / CONTRACTED)
    return (1.0 + 2.0 * jnp.cos(phase)) / BEADS


def first_kernel(ring, centroid_ref, offsets_ref, q_ref, *part_refs):
    table = shares(ring, offsets_ref.shape[1], 1)
    for c in range(3):
        scaled = centroid_ref[c : c + 1, :] * f32(SLAB_SIDE if c else 1.0)
        q = scaled + offsets_ref[c]
        q_ref[c] = q
        for d in range(ring):
            part_refs[d][c : c + 1, :] = jnp.sum(table[:, d : d + 1] * q, axis=0, keepdims=True)


def first_step(centroid, offsets, ring):
    part = jax.ShapeDtypeStruct(centroid.shape, f32)
    return pl.pallas_call(
        functools.partial(first_kernel, ring),
        out_shape=(jax.ShapeDtypeStruct(offsets.shape, f32),) + (part,) * ring,
        in_specs=[pl.BlockSpec(memory_space=VMEM)] * 2,
        out_specs=(pl.BlockSpec(memory_space=VMEM),) * (1 + ring),
        compiler_params=pltpu.CompilerParams(vmem_limit_bytes=8 << 20),
        cost_estimate=pl.CostEstimate(flops=1 << 28, bytes_accessed=1 << 19, transcendentals=0),
    )(centroid, offsets)


def last_kernel(ring, force_ref, react_ref, *refs):
    table = shares(ring, force_ref.shape[1], -1) * f32(BEADS / CONTRACTED)
    *many_refs, out_ref = refs
    for c in range(3):
        total = force_ref[c] + react_ref[c]
        for d in range(ring):
            total = total + table[:, d : d + 1] * many_refs[d][c : c + 1, :]
        out_ref[c] = total


def last_step(force, react, many):
    return pl.pallas_call(
        functools.partial(last_kernel, len(many)),
        out_shape=jax.ShapeDtypeStruct(force.shape, f32),
        in_specs=[pl.BlockSpec(memory_space=VMEM)] * (2 + len(many)),
        out_specs=pl.BlockSpec(memory_space=VMEM),
        compiler_params=pltpu.CompilerParams(vmem_limit_bytes=8 << 20),
        cost_estimate=pl.CostEstimate(flops=1 << 28, bytes_accessed=1 << 19, transcendentals=0),
    )(force, react, *many)


def shards(centroid, bead_offsets, routes):
    beads_dev, _, mols = bead_offsets.shape
    domains = lax.axis_size("space")
    ring = lax.axis_size("bead")
    capacity = 2 * mols // domains
    half = beads_dev // 2
    q, *parts = first_step(centroid, bead_offsets.transpose(1, 0, 2), ring)
    nxt = passed_along(q, "space", -1)
    parts = parts[:1] + [passed_along(parts[by], "bead", by) for by in range(1, ring)]

    force = self_pairs(q, None, 0, half)
    route = routes.reshape(1, mols)
    outbox, slot = routed(parts, route, domains, capacity, force)
    inbox = lax.all_to_all(outbox, "space", split_axis=0, concat_axis=0, tiled=True)
    force, react = cross_pairs(q, nxt, force, jnp.zeros_like(q), 0, half, (outbox,))
    bodies = body_forces(inbox, force)
    returned = lax.all_to_all(bodies, "space", split_axis=0, concat_axis=0, tiled=True)
    force, react = cross_pairs(q, nxt, force, react, half, half, (bodies,))
    mine = unrouted(returned, route, slot, force)
    arrived = passed_along(react, "space", 1)
    every = [mine] + [passed_along(mine, "bead", by) for by in range(1, ring)]
    force = self_pairs(q, force, half, half, (mine,))
    return last_step(force, arrived, every).transpose(1, 0, 2)


def solution(mesh):
    placed = (P(None, "space"), P("bead", None, "space"), P("space", None))
    return jax.shard_map(
        shards, mesh=mesh, in_specs=placed, out_specs=P("bead", None, "space"), check_vma=False
    )
```
